256 devices in a mesh: fsdp: 16 (over x_lo, z), expert: 16 (over y, x_hi, core).
Axes of the slice: x: 4 (x_hi: 2, x_lo: 2; x = x_hi * 2 + x_lo), y: 4, z: 8, core: 2. Of those that a mesh axis runs over, the one named last changes fastest.
Arguments:
- tokens: bfloat16 [2048, 3072], P('expert'), may hold values from -6 to 6
- cotangent: bfloat16 [2048, 3072], P('expert'), may hold values from -6 to 6
- expert_ids: int32 [2048, 4], P('expert'), may hold values from 0 to 15, all different within a row; in each aligned block of 128 rows (0 to 127, 128 to 255, ...) at most 40 rows name the same one
- gate_values: bfloat16 [2048, 4], P('expert'), may hold values from 0.049804688 to 0.5
- w_in: bfloat16 [3072, 16, 6144], P(None, 'expert', 'fsdp'), may hold values from -0.109375 to 0.109375
- w_out: bfloat16 [6144, 16, 3072], P('fsdp', 'expert'), may hold values from -0.078125 to 0.078125
Outputs:
- grad_tokens: bfloat16 [2048, 3072], P('expert')
- grad_gates: bfloat16 [2048, 4], P('expert')
- grad_w_in: bfloat16 [3072, 16, 6144], P(None, 'expert', 'fsdp')
- grad_w_out: bfloat16 [6144, 16, 3072], P('fsdp', 'expert')
The draws below stay inside these ranges and needn't reach their ends.
Inputs may be any that keep to these rules, and one draw needn't show every extreme that they name: `expert_ids`: in each aligned block of 128 rows (the rows of one index of the expert axis) the 4 entries of a row differ, no expert is named by more than 40 rows, a bound that some block reaches.
All inputs are finite; a program needn't handle non-finite values.
Results may differ from the reference program's by a relative error of at most 0.0049.
Values may be sent and summed in bfloat16 or wider, within the bound.
A program may use at most 128 MiB of HBM per device.

```python
import math
import jax
import jax.numpy as jnp
import numpy as np
from jax import lax

D = 3072
FF = 6144
EXPERTS = 16
TOP = 4
TOK_DEV = 128
CAP = 40
TOKENS = 2048
N_EXPERT = 16


def level_of(rng, shape, split, least, high):
    gain, own = 1.0, jax.random.fold_in(rng, 6)
    for dim, shards_of in split:
        draws = jnp.exp(jax.random.uniform(jax.random.fold_in(own, dim), (shards_of,), jnp.float32, least / len(split), high / len(split)))
        gain = gain * jnp.repeat(draws, shape[dim] // shards_of).reshape([-1 if axis == dim else 1 for axis in range(len(shape))])
    return gain


def assign_block(key, own, number, rows, amount, top, most, slope):
    ranking = jax.random.permutation(key, amount)
    packed, common = load_shares(amount, rows * top, most, slope, True), load_shares(amount, rows * top, most, slope, False)
    places = jnp.arange(amount)

    def named(lengths, turn):
        used = int((lengths > 0).sum())
        fixed = max(1, used // 4)
        moved = fixed + (places - fixed + turn * (used - fixed)) % max(1, amount - fixed)
        return jnp.zeros((amount,), jnp.int32).at[ranking[jnp.where(places < fixed, places, moved)]].set(jnp.asarray(lengths, jnp.int32))

    lengths = jnp.where(number % 4 == 0, named(packed, number // 4), named(common, number - number // 4 - 1))
    mixed = jax.random.permutation(jax.random.fold_in(own, 3), amount)
    donor, sink = mixed[0:amount // 2 * 2:2], mixed[1:amount // 2 * 2:2]
    slack = jnp.minimum(lengths[donor] - 1, most - lengths[sink]) // 2
    slack = jnp.where((donor == ranking[0]) | (sink == ranking[0]) | (lengths[sink] == 0), 0, jnp.maximum(slack, 0))
    moved = jax.random.randint(jax.random.fold_in(own, 4), (amount // 2,), 0, 1 << 20) % (slack + 1)
    lengths = lengths.at[donor].add(-moved).at[sink].add(moved)
    labels = jnp.searchsorted(jnp.cumsum(lengths), jnp.arange(rows * top), side="right").astype(jnp.int32)
    grid = labels.reshape(top, rows).T
    grid = grid[jax.random.permutation(jax.random.fold_in(own, 1), rows)]
    turn = jax.random.randint(jax.random.fold_in(own, 2), (rows, 1), 0, top)
    return jnp.take_along_axis(grid, (jnp.arange(top)[None, :] + turn) % top, axis=1)


def load_shares(count, total, bound, skew, full):
    loads = [(1 << 20) // math.isqrt(standing ** skew) + 1 for standing in range(1, count + 1)]
    largest = bound if full else min(bound, max(-(-total // count), total * loads[0] // sum(loads)))
    least = 1 if total - largest >= count - 1 else 0
    counts, rest = [largest] + [least] * (count - 1), total - largest - least * (count - 1)
    while rest > 0:
        candidates = [i for i in range(1, count) if counts[i] < largest] or [i for i in range(1, count) if counts[i] < bound]
        whole, remaining = sum([loads[i] for i in candidates]), rest
        for i in candidates:
            addition = min(bound - counts[i], max(1, remaining * loads[i] // whole), rest)
            counts[i] = counts[i] + addition
            rest = rest - addition
    return np.array(counts)


def scatter_about(rng, shape, deviation, bound, cuts=(), held_as=jnp.bfloat16):
    factor_of = level_of(rng, shape, cuts, -0.22, 0.18) if cuts else 1.0
    result = jax.random.normal(rng, shape, jnp.float32) * deviation * factor_of
    return jnp.minimum(jnp.maximum(result, -bound), bound).astype(held_as)


def setup_inputs(seed: int = 0) -> dict:
    splits = jax.random.split(jax.random.key(seed), 7)
    tokens = scatter_about(splits[0], (TOKENS, D), 1.0, 6.0, ((0, 16),))
    cotangent = scatter_about(splits[1], (TOKENS, D), 1.0, 6.0, ((0, 16),))
    expert_ids_keys = jax.random.split(jax.random.fold_in(splits[2], 1), TOKENS // TOK_DEV)
    expert_ids_turns = jax.random.permutation(jax.random.fold_in(splits[2], 3), TOKENS // TOK_DEV)
    expert_ids = jax.vmap(lambda own, number: assign_block(jax.random.fold_in(splits[2], 2), own, number, TOK_DEV, EXPERTS, TOP, CAP, 1))(expert_ids_keys, expert_ids_turns).reshape((TOKENS, TOP))
    gate_values = jnp.clip(0.049804688 + 0.4501953 * jax.random.uniform(splits[3], (TOKENS, TOP), jnp.float32) ** level_of(splits[3], (TOKENS, TOP), ((0, 16),), -0.2, 0.2), 0.049804688, 0.5).astype(jnp.bfloat16)
    w_in = scatter_about(splits[4], (D, EXPERTS, FF), D ** -0.5, 0.109375, ((1, 16), (2, 16)))
    w_out = scatter_about(splits[5], (FF, EXPERTS, D), FF ** -0.5, 0.078125, ((0, 16), (1, 16)))
    return {"tokens": tokens, "cotangent": cotangent, "expert_ids": expert_ids, "gate_values": gate_values, "w_in": w_in, "w_out": w_out}


def slot_targets(expert_ids):
    flat = expert_ids.reshape(-1).astype(jnp.int32)
    table = (flat[:, None] == jnp.arange(EXPERTS, dtype=jnp.int32)[None, :]).astype(jnp.int32)
    earlier = jnp.cumsum(table, axis=0) - table
    position = jnp.sum(earlier * table, axis=1).astype(jnp.int32)
    return (flat * CAP + position).astype(jnp.int32)


def fill_slots(rows, target):
    holder = jnp.zeros((EXPERTS * CAP,) + rows.shape[1:], rows.dtype)
    return holder.at[target].set(rows)


def token_slots(rows, target):
    return fill_slots(jnp.repeat(rows, TOP, axis=0), target)


def gate_slots(gates, target):
    return fill_slots(gates.reshape(-1), target)


def pick_rows(lookup, target):
    return lookup[target]


def one_expert(inputs):
    x_rows, g_rows, gate_rows, in_proj, out_proj = inputs
    pre_act = jnp.dot(x_rows, in_proj, preferred_element_type=jnp.float32)
    upstream = jnp.dot(g_rows, out_proj.T, preferred_element_type=jnp.float32)
    squash = jax.nn.sigmoid(pre_act)
    active = pre_act * squash
    gate_grad = jnp.sum(active * upstream, axis=-1)
    gate_col = gate_rows.astype(jnp.float32)[:, None]
    act_gated = (gate_col * active).astype(jnp.bfloat16)
    grad_pre = (gate_col * squash * (1.0 + pre_act * (1.0 - squash)) * upstream).astype(jnp.bfloat16)
    grad_x = jnp.dot(grad_pre, in_proj.T, preferred_element_type=jnp.float32)
    grad_in = jnp.dot(x_rows.T, grad_pre, preferred_element_type=jnp.float32).astype(jnp.bfloat16)
    grad_out = jnp.dot(act_gated.T, g_rows, preferred_element_type=jnp.float32).astype(jnp.bfloat16)
    return grad_x, gate_grad, grad_in, grad_out


def reference(tokens, cotangent, expert_ids, gate_values, w_in, w_out):
    blocks = N_EXPERT
    tok_blocks = tokens.reshape(blocks, TOK_DEV, D)
    cot_blocks = cotangent.reshape(blocks, TOK_DEV, D)
    id_blocks = expert_ids.reshape(blocks, TOK_DEV, TOP)
    gate_blocks = gate_values.reshape(blocks, TOK_DEV, TOP)
    target = jax.vmap(slot_targets)(id_blocks)
    x_slot = jax.vmap(token_slots)(tok_blocks, target).reshape(blocks, EXPERTS, CAP, D)
    g_slot = jax.vmap(token_slots)(cot_blocks, target).reshape(blocks, EXPERTS, CAP, D)
    gate_slot = jax.vmap(gate_slots)(gate_blocks, target).reshape(blocks, EXPERTS, CAP)
    x_exp = jnp.transpose(x_slot, (1, 0, 2, 3)).reshape(EXPERTS, blocks * CAP, D)
    g_exp = jnp.transpose(g_slot, (1, 0, 2, 3)).reshape(EXPERTS, blocks * CAP, D)
    gate_exp = jnp.transpose(gate_slot, (1, 0, 2)).reshape(EXPERTS, blocks * CAP)
    in_stack = jnp.moveaxis(w_in, 1, 0)
    out_stack = jnp.moveaxis(w_out, 1, 0)
    grad_x, gate_grad, grad_in, grad_out = lax.map(one_expert, (x_exp, g_exp, gate_exp, in_stack, out_stack))
    grad_x = jnp.transpose(grad_x.reshape(EXPERTS, blocks, CAP, D), (1, 0, 2, 3)).reshape(blocks, EXPERTS * CAP, D)
    gate_grad = jnp.transpose(gate_grad.reshape(EXPERTS, blocks, CAP), (1, 0, 2)).reshape(blocks, EXPERTS * CAP)
    picked = jax.vmap(pick_rows)(grad_x, target).reshape(blocks, TOK_DEV, TOP, D)
    grad_tokens = picked.sum(axis=2).astype(jnp.bfloat16).reshape(TOKENS, D)
    picked_gate = jax.vmap(pick_rows)(gate_grad, target)
    grad_gates = picked_gate.astype(jnp.bfloat16).reshape(TOKENS, TOP)
    grad_w_in = jnp.moveaxis(grad_in, 0, 1)
    grad_w_out = jnp.moveaxis(grad_out, 0, 1)
    return grad_tokens, grad_gates, grad_w_in, grad_w_out
```

```python
import jax
import jax.numpy as jnp
from jax import lax
from jax.sharding import PartitionSpec as P

EXPERTS = 16
CAP = 40
F32 = jnp.float32
BF16 = jnp.bfloat16


def local(tokens, cotangent, expert_ids, gate_values, w_in, w_out):
    rows, width = tokens.shape
    n_f = lax.axis_size("fsdp")
    part = 2 * width // n_f
    me_f = lax.axis_index("fsdp")
    half = me_f // (n_f // 2)
    col = (me_f % (n_f // 2)) * part

    ids_t = expert_ids.T
    experts = jnp.arange(EXPERTS, dtype=jnp.int32)[:, None]
    hit = ids_t[None] == experts[:, :, None]
    named = jnp.any(hit, axis=1)
    gates_of = jnp.sum(jnp.where(hit, gate_values.T[None].astype(F32), 0.0), axis=1)
    before = jnp.arange(rows)[:, None] < jnp.arange(rows)[None, :]
    place = jnp.dot(
        named.astype(BF16), before.astype(BF16), preferred_element_type=F32
    ).astype(jnp.int32)
    slots = jnp.arange(CAP, dtype=jnp.int32)[None, :, None]
    pick = ((place[:, None, :] == slots) & named[:, None, :]).reshape(EXPERTS * CAP, rows)
    pick_b = pick.astype(BF16)
    gate_send = jnp.sum(
        jnp.where(pick.reshape(EXPERTS, CAP, rows), gates_of[:, None, :], 0.0), axis=2
    )

    chosen = jnp.where(half == 0, lax.dynamic_slice_in_dim(tokens, col, part, 1),
                       lax.dynamic_slice_in_dim(cotangent, col, part, 1))
    send = jnp.dot(pick_b, chosen, preferred_element_type=F32).astype(BF16)
    send = send.reshape(EXPERTS, CAP, part)
    got = lax.all_to_all(send, "expert", split_axis=0, concat_axis=0, tiled=True)
    gate_got = lax.all_to_all(gate_send, "expert", split_axis=0, concat_axis=0, tiled=True)
    every = lax.all_gather(got.reshape(EXPERTS * CAP, part), "fsdp", axis=0)
    xs, gs = every[: n_f // 2], every[n_f // 2 :]
    win = w_in.reshape(n_f // 2, part, -1)
    wout = w_out.reshape(-1, n_f // 2, part)
    pre = jnp.einsum("zsd,zdf->sf", xs, win, preferred_element_type=F32)
    up = jnp.einsum("zsd,fzd->sf", gs, wout, preferred_element_type=F32)
    gate = gate_got.reshape(EXPERTS * CAP, 1)
    squash = jax.nn.sigmoid(pre)
    active = pre * squash
    gate_part = jnp.sum(active * up, axis=-1)
    act_gated = (gate * active).astype(BF16)
    grad_pre = (gate * squash * (1.0 + pre * (1.0 - squash)) * up).astype(BF16)
    w16 = w_in.reshape(n_f, width // n_f, -1)
    part_x = jnp.einsum("sf,zdf->zsd", grad_pre, w16, preferred_element_type=F32)
    mine = lax.psum_scatter(part_x, "fsdp", scatter_dimension=0, tiled=False)
    gate_sum = lax.psum(gate_part.reshape(EXPERTS, CAP), "fsdp")
    back_x = lax.all_to_all(mine.reshape(EXPERTS, CAP, -1), "expert", 0, 0, tiled=True)
    back_gate = lax.all_to_all(gate_sum, "expert", split_axis=0, concat_axis=0, tiled=True)
    grad_in = jnp.einsum("zsd,sf->zdf", xs, grad_pre, preferred_element_type=F32).astype(BF16)
    grad_out = jnp.einsum("sf,zsd->fzd", act_gated, gs, preferred_element_type=F32).astype(BF16)
    tok = jnp.dot(
        pick.astype(F32).T, back_x.reshape(EXPERTS * CAP, -1),
        precision=lax.Precision.HIGHEST, preferred_element_type=F32,
    ).astype(BF16)
    grad_tokens = lax.all_gather(tok, "fsdp", axis=1, tiled=True)
    by_expert = jnp.sum(
        jnp.where(pick.reshape(EXPERTS, CAP, rows), back_gate[:, :, None], 0.0), axis=1
    )
    grad_gates = jnp.sum(jnp.where(hit, by_expert[:, None, :], 0.0), axis=0).T.astype(BF16)
    return (
        grad_tokens,
        grad_gates,
        grad_in.reshape(w_in.shape),
        grad_out.reshape(w_out.shape),
    )


def solution(mesh):
    return jax.shard_map(
        local,
        mesh=mesh,
        in_specs=(
            P("expert", None),
            P("expert", None),
            P("expert", None),
            P("expert", None),
            P(None, "expert", "fsdp"),
            P("fsdp", "expert", None),
        ),
        out_specs=(
            P("expert", None),
            P("expert", None),
            P(None, "expert", "fsdp"),
            P("fsdp", "expert", None),
        ),
        check_vma=False,
    )
```

```python
import functools

import jax
import jax.numpy as jnp
from jax import lax
from jax.experimental import pallas as pl
from jax.experimental.pallas import tpu as pltpu
from jax.sharding import PartitionSpec as P

CAP = 40
F32 = jnp.float32
BF16 = jnp.bfloat16
MESH = pl.DeviceIdType.MESH
LANE = 128


def nt(a, b):
    return lax.dot_general(a, b, (((1,), (1,)), ((), ())), preferred_element_type=F32)


def tn(a, b):
    return lax.dot_general(a, b, (((0,), (0,)), ((), ())), preferred_element_type=F32)


def flat(v):
    return v.astype(F32).reshape(v.shape[0] * v.shape[1], v.shape[2]).astype(BF16)


def blocks(v):
    return v.reshape(v.shape[0] // CAP, CAP, v.shape[1])


def kernel(
    nf, ne, tok_ref, cot_ref, ids_ref, gates_ref, win_hbm, wout_hbm,
    out_ref, ogate_ref, gin_hbm, gout_hbm,
    win, wout, sel32, sel, x2, g2, send_x, x_all, send_g, g_all, pre, gp16, ag16,
    rs_send, rs_recv, back_send, back_recv, pair_send, pair_recv, tok_all,
    gs_send, gs_recv, gf_all, gin, gout,
    load_sem, x_ss, x_rs, g_ss, g_rs, xr_ss, xr_rs, rs_ss, rs_rs, bk_ss, bk_rs,
    pr_ss, pr_rs, tr_ss, tr_rs, gs_ss, gs_rs, gf_ss, gf_rs, st_sem,
):
    me_f, me_e = lax.axis_index("fsdp"), lax.axis_index("expert")
    nz = nf // 2
    lo, z = me_f // nz, me_f % nz
    rows, width = tok_ref.shape
    wz = width // nz
    ff = win.shape[1]
    top = ids_ref.shape[0]
    slots = ne * CAP
    he, hs = ne // 2, slots // 2
    pair_f = (1 - lo) * nz + z
    right_f = lo * nz + (z + 1) % nz
    left_f = lo * nz + (z + nz - 1) % nz

    def dev(f, e):
        return {"fsdp": f, "expert": e}

    def remote(src, dst, ss, rs, f, e):
        return pltpu.make_async_remote_copy(
            src_ref=src, dst_ref=dst, send_sem=ss, recv_sem=rs,
            device_id=dev(f, e), device_id_type=MESH,
        )

    barrier = pltpu.get_barrier_semaphore()

    def greet_e(k, c):
        pl.semaphore_signal(barrier, inc=1, device_id=dev(me_f, (me_e + k) % ne), device_id_type=MESH)
        return c

    def greet_f(k, c):
        pl.semaphore_signal(barrier, inc=1, device_id=dev((me_f + k) % nf, me_e), device_id_type=MESH)
        return c

    lax.fori_loop(1, ne, greet_e, 0)
    lax.fori_loop(1, nf, greet_f, 0)
    load_in = pltpu.make_async_copy(win_hbm, win, load_sem.at[0])
    load_out = pltpu.make_async_copy(wout_hbm, wout, load_sem.at[1])
    load_in.start()
    load_out.start()

    ids = ids_ref[...]
    gates = gates_ref[...].astype(F32)
    exps = lax.broadcasted_iota(jnp.int32, (ne, rows), 0)
    named = jnp.zeros((ne, rows), F32)
    gate_of = jnp.zeros((ne, rows), F32)
    for k in range(top):
        hit = exps == ids[k : k + 1, :]
        named = named + jnp.where(hit, 1.0, 0.0)
        gate_of = gate_of + jnp.where(hit, gates[k : k + 1, :], 0.0)
    before = lax.broadcasted_iota(jnp.int32, (rows, rows), 0) < lax.broadcasted_iota(
        jnp.int32, (rows, rows), 1
    )
    place = jnp.dot(
        named.astype(BF16), jnp.where(before, 1.0, 0.0).astype(BF16), preferred_element_type=F32
    )
    place = jnp.where(named > 0.5, place, -1.0)
    slot_no = lax.broadcasted_iota(jnp.int32, (CAP, rows), 0).astype(F32)
    for e in range(ne):
        one = jnp.where(slot_no == place[e : e + 1, :], 1.0, 0.0)
        sel32[e] = one
        gate_col = jnp.sum(one * gate_of[e : e + 1, :], axis=1, keepdims=True)
        send_g[e, :, width:] = jnp.broadcast_to(gate_col, (CAP, LANE)).astype(BF16)
    sel[...] = sel32[...].reshape(slots, rows).astype(BF16)
    pick = sel[...]
    cols = pl.ds(pl.multiple_of(z * wz, LANE), wz)
    send_x[...] = blocks(jnp.dot(pick, tok_ref[:, cols], preferred_element_type=F32)).astype(BF16)

    pl.semaphore_wait(barrier, (ne - 1) + (nf - 1))

    def x_copy(k):
        e = (me_e + k) % ne
        return remote(send_x.at[e], x_all.at[z, me_e], x_ss.at[e], x_rs.at[me_e], me_f, e)

    def x_start(k, c):
        x_copy(k).start()
        return c

    lax.fori_loop(1, ne, x_start, 0)
    own_x = pltpu.make_async_copy(send_x.at[me_e], x_all.at[z, me_e], st_sem.at[0])
    own_x.start()

    gw = width // 6 if width % (6 * LANE) == 0 else width

    def g_build(j, c):
        span = pl.ds(pl.multiple_of(j * gw, LANE), gw)
        send_g[:, :, span] = blocks(
            jnp.dot(sel[...], cot_ref[:, span], preferred_element_type=F32)
        ).astype(BF16)
        return c

    lax.fori_loop(0, width // gw, g_build, 0)

    def g_start(k, c):
        e = (me_e + k) % ne
        remote(send_g.at[e], g_all.at[me_e], g_ss.at[e], g_rs.at[me_e], me_f, e).start()
        return c

    lax.fori_loop(1, ne, g_start, 0)
    own_g = pltpu.make_async_copy(send_g.at[me_e], g_all.at[me_e], st_sem.at[1])
    own_g.start()

    def x_wait(k, c):
        b = (me_e + ne - k) % ne
        remote(send_x.at[b], x_all.at[z, b], x_ss.at[b], x_rs.at[b], me_f, b).wait_recv()
        return c

    lax.fori_loop(1, ne, x_wait, 0)
    own_x.wait()

    far = nz // 2

    def hops(direction, h):
        return far if direction == h else far - 1

    def ring_copy(buf, lead, ss, rs, direction, h, i):
        piece = (z + nz - i) % nz if direction == 0 else (z + i) % nz
        ref = lead(buf, piece, h)
        return remote(
            ref, ref, ss.at[direction, h, i], rs.at[direction, h, i],
            right_f if direction == 0 else left_f, me_e,
        )

    def ring_arrival(buf, lead, ss, rs, direction, h, i):
        piece = (z + nz - 1 - i) % nz if direction == 0 else (z + 1 + i) % nz
        ref = lead(buf, piece, h)
        return remote(
            ref, ref, ss.at[direction, h, i], rs.at[direction, h, i],
            right_f if direction == 0 else left_f, me_e,
        )

    def ring(buf, lead, ss, rs, between):
        for i in range(far + 1):
            for h in (0, 1):
                for d in (0, 1):
                    if 0 < i <= hops(d, h):
                        ring_arrival(buf, lead, ss, rs, d, h, i - 1).wait_recv()
                    if i < hops(d, h):
                        ring_copy(buf, lead, ss, rs, d, h, i).start()
            between(i)

    def ring_drain(buf, lead, ss, rs):
        for i in range(far):
            for h in (0, 1):
                for d in (0, 1):
                    if i < hops(d, h):
                        ring_copy(buf, lead, ss, rs, d, h, i).wait_send()

    def x_lead(buf, piece, h):
        return buf.at[piece, pl.ds(h * he, he)]

    def add_pre(c):
        w_rows = win[pl.ds(pl.multiple_of(c * wz, LANE), wz), :]
        for h in (0, 1):
            xs = flat(x_all[c, h * he : (h + 1) * he])
            x2[c, h * hs : (h + 1) * hs, :] = xs
            pre[h * hs : (h + 1) * hs, :] += jnp.dot(xs, w_rows, preferred_element_type=F32)

    pre[...] = jnp.zeros_like(pre)

    def x_between(i):
        if i == 0:
            load_in.wait()
            add_pre(z)
            return
        add_pre((z + nz - i) % nz)
        if i < far:
            add_pre((z + i) % nz)

    ring(x_all, x_lead, xr_ss, xr_rs, x_between)

    def g_arrival(b):
        return remote(send_g.at[b], g_all.at[b], g_ss.at[b], g_rs.at[b], me_f, b)

    def g_flat(p):
        g2[pl.ds(pl.multiple_of(p * 2 * CAP, 16), 2 * CAP), :] = flat(
            g_all[pl.ds(2 * p, 2), :, :width]
        )

    own_g.wait()
    g_arrival(me_e + 1 - 2 * (me_e % 2)).wait_recv()
    g_flat(me_e // 2)

    def g_take(k, c):
        p = (me_e // 2 + he - k) % he
        g_arrival(2 * p).wait_recv()
        g_arrival(2 * p + 1).wait_recv()
        g_flat(p)
        return c

    lax.fori_loop(1, he, g_take, 0)
    load_out.wait()

    for h in (0, 1):
        span = slice(h * hs, (h + 1) * hs)
        up = nt(g2[span, :], wout[...])
        gate = g_all[h * he : (h + 1) * he, :, width:].astype(F32).reshape(hs, LANE)
        gate = jnp.concatenate([gate] * (ff // LANE), axis=1)
        p = pre[span, :]
        squash = jax.nn.sigmoid(p)
        active = p * squash
        part = jnp.sum(active * up, axis=1, keepdims=True)
        gs_send[h * he : (h + 1) * he] = blocks(jnp.broadcast_to(part, (hs, LANE)))
        ag16[span, :] = (gate * active).astype(BF16)
        gp16[span, :] = (gate * squash * (1.0 + p * (1.0 - squash)) * up).astype(BF16)

    def share(c, h):
        return blocks(
            nt(gp16[h * hs : (h + 1) * hs, :], win[pl.ds(pl.multiple_of(c * wz, LANE), wz), :])
        )

    def rs_src(d, h, i):
        return rs_send.at[d, h] if i == 0 else rs_recv.at[d, h, i - 1]

    def rs_copy(d, h, i):
        return remote(
            rs_src(d, h, i), rs_recv.at[d, h, i], rs_ss.at[d, h, i], rs_rs.at[d, h, i],
            right_f if d == 0 else left_f, me_e,
        )

    def rs_step(d, h, i):
        n = hops(d, h)
        c = (z + n - i) % nz if d == 0 else (z + nz - (n - i)) % nz
        total = share(c, h)
        if i > 0:
            rs_copy(d, h, i - 1).wait_recv()
            total = total + rs_src(d, h, i)[...].astype(F32)
        rs_src(d, h, i)[...] = total.astype(BF16)
        rs_copy(d, h, i).start()

    def gs_start(k, c):
        e = (me_e + k) % ne
        remote(gs_send.at[e], gs_recv.at[me_e], gs_ss.at[e], gs_rs.at[me_e], me_f, e).start()
        return c

    def gs_wait(k, c):
        b = (me_e + ne - k) % ne
        remote(gs_send.at[b], gs_recv.at[b], gs_ss.at[b], gs_rs.at[b], me_f, b).wait_recv()
        return c

    def grad_in_piece(c):
        gin[pl.ds(pl.multiple_of(c * wz, LANE), wz), :] = tn(
            x2[c], gp16[...]
        ).astype(BF16)

    def grad_out_piece(c):
        span = pl.ds(pl.multiple_of(c * wz, LANE), wz)
        gout[:, span] = tn(
            ag16[...], g2[:, span]
        ).astype(BF16)

    def grads(first, last):
        def one(c, carry):
            grad_in_piece(c)
            grad_out_piece(c)
            return carry

        lax.fori_loop(first, last, one, 0)

    def gates_pass():
        lax.fori_loop(1, ne, gs_wait, 0)
        own_gs.wait()
        acc = jnp.zeros((top, rows), F32)
        for e in range(ne):
            row = jnp.sum(sel32[e] * gs_recv[e], axis=0, keepdims=True)
            acc = acc + jnp.where(ids_ref[...] == e, row, 0.0)
        gf_all[me_f, :top, :] = acc

        def gf_start(k, c):
            f = (me_f + k) % nf
            remote(gf_all.at[me_f], gf_all.at[me_f], gf_ss.at[f], gf_rs.at[me_f], f, me_e).start()
            return c

        lax.fori_loop(1, nf, gf_start, 0)

    own_gs = pltpu.make_async_copy(gs_send.at[me_e], gs_recv.at[me_e], st_sem.at[2])
    for i in range(far):
        for h in (0, 1):
            for d in (0, 1):
                if i < hops(d, h):
                    rs_step(d, h, i)
        if i == 0:
            lax.fori_loop(1, ne, gs_start, 0)
            own_gs.start()
        grads(i * nz // far, (i + 1) * nz // far)
        if i == 0:
            gates_pass()
    store_in = pltpu.make_async_copy(gin, gin_hbm, st_sem.at[3])
    store_out = pltpu.make_async_copy(gout, gout_hbm, st_sem.at[4])
    store_in.start()
    store_out.start()

    def back_start(k, c):
        e = (me_e + k) % ne
        remote(back_send.at[e], back_recv.at[me_e], bk_ss.at[e], bk_rs.at[me_e], me_f, e).start()
        return c

    def back_wait(k, c):
        b = (me_e + ne - k) % ne
        remote(back_send.at[b], back_recv.at[b], bk_ss.at[b], bk_rs.at[b], me_f, b).wait_recv()
        return c

    for h in (0, 1):
        total = share(z, h)
        for d in (0, 1):
            last = hops(d, h) - 1
            rs_copy(d, h, last).wait_recv()
            total = total + rs_recv[d, h, last].astype(F32)
        back_send[h * he : (h + 1) * he] = total.astype(BF16)
    lax.fori_loop(1, ne, back_start, 0)
    own_back = pltpu.make_async_copy(back_send.at[me_e], back_recv.at[me_e], st_sem.at[5])
    own_back.start()

    def gf_wait(k, c):
        f = (me_f + nf - k) % nf
        remote(gf_all.at[f], gf_all.at[f], gf_ss.at[f], gf_rs.at[f], f, me_e).wait_recv()
        return c

    lax.fori_loop(1, nf, gf_wait, 0)
    total_gate = gf_all[0, :top, :]
    for f in range(1, nf):
        total_gate = total_gate + gf_all[f, :top, :]
    ogate_ref[...] = total_gate.astype(BF16)

    lax.fori_loop(1, ne, back_wait, 0)
    own_back.wait()
    tok = tn(sel[...], flat(back_recv[...]))
    pair_send[...] = tok.astype(BF16)
    pair = remote(pair_send, pair_recv, pr_ss, pr_rs, pair_f, me_e)
    pair.start()
    pair.wait_recv()
    tok_all[z] = (pair_send[...].astype(F32) + pair_recv[...].astype(F32)).astype(BF16)

    hr = rows // 2

    def t_lead(buf, piece, h):
        return buf.at[piece, pl.ds(h * hr, hr)]

    ring(tok_all, t_lead, tr_ss, tr_rs, lambda i: None)
    for c in range(nz):
        out_ref[:, c * wz : (c + 1) * wz] = tok_all[c]

    def drain(k, c):
        e = (me_e + k) % ne
        remote(send_x.at[e], x_all.at[z, me_e], x_ss.at[e], x_rs.at[me_e], me_f, e).wait_send()
        remote(send_g.at[e], g_all.at[me_e], g_ss.at[e], g_rs.at[me_e], me_f, e).wait_send()
        remote(gs_send.at[e], gs_recv.at[me_e], gs_ss.at[e], gs_rs.at[me_e], me_f, e).wait_send()
        remote(back_send.at[e], back_recv.at[me_e], bk_ss.at[e], bk_rs.at[me_e], me_f, e).wait_send()
        return c

    def drain_f(k, c):
        f = (me_f + k) % nf
        remote(gf_all.at[me_f], gf_all.at[me_f], gf_ss.at[f], gf_rs.at[me_f], f, me_e).wait_send()
        return c

    lax.fori_loop(1, ne, drain, 0)
    lax.fori_loop(1, nf, drain_f, 0)
    ring_drain(x_all, x_lead, xr_ss, xr_rs)
    ring_drain(tok_all, t_lead, tr_ss, tr_rs)
    for i in range(far):
        for h in (0, 1):
            for d in (0, 1):
                if i < hops(d, h):
                    rs_copy(d, h, i).wait_send()
    pair.wait_send()
    store_in.wait()
    store_out.wait()


def local(nf, ne, tokens, cotangent, expert_ids, gate_values, w_in, w_out):
    rows, width = tokens.shape
    top = expert_ids.shape[1]
    ff = w_in.shape[2]
    nz = nf // 2
    wz = width // nz
    far = nz // 2
    he = ne // 2
    dma = pltpu.SemaphoreType.DMA
    vmem = pl.BlockSpec(memory_space=pltpu.VMEM)
    hbm = pl.BlockSpec(memory_space=pl.ANY)
    ring_sems = dma((2, 2, far))
    out = pl.pallas_call(
        functools.partial(kernel, nf, ne),
        out_shape=(
            jax.ShapeDtypeStruct((rows, width), BF16),
            jax.ShapeDtypeStruct((top, rows), BF16),
            jax.ShapeDtypeStruct((width, ff), BF16),
            jax.ShapeDtypeStruct((ff, width), BF16),
        ),
        in_specs=[vmem, vmem, vmem, vmem, hbm, hbm],
        out_specs=(vmem, vmem, hbm, hbm),
        scratch_shapes=[
            pltpu.VMEM((width, ff), BF16),
            pltpu.VMEM((ff, width), BF16),
            pltpu.VMEM((ne, CAP, rows), F32),
            pltpu.VMEM((ne * CAP, rows), BF16),
            pltpu.VMEM((nz, ne * CAP, wz), BF16),
            pltpu.VMEM((ne * CAP, width), BF16),
            pltpu.VMEM((ne, CAP, wz), BF16),
            pltpu.VMEM((nz, ne, CAP, wz), BF16),
            pltpu.VMEM((ne, CAP, width + LANE), BF16),
            pltpu.VMEM((ne, CAP, width + LANE), BF16),
            pltpu.VMEM((ne * CAP, ff), F32),
            pltpu.VMEM((ne * CAP, ff), BF16),
            pltpu.VMEM((ne * CAP, ff), BF16),
            pltpu.VMEM((2, 2, he, CAP, wz), BF16),
            pltpu.VMEM((2, 2, far, he, CAP, wz), BF16),
            pltpu.VMEM((ne, CAP, wz), BF16),
            pltpu.VMEM((ne, CAP, wz), BF16),
            pltpu.VMEM((rows, wz), BF16),
            pltpu.VMEM((rows, wz), BF16),
            pltpu.VMEM((nz, rows, wz), BF16),
            pltpu.VMEM((ne, CAP, LANE), F32),
            pltpu.VMEM((ne, CAP, LANE), F32),
            pltpu.VMEM((nf, 8, rows), F32),
            pltpu.VMEM((width, ff), BF16),
            pltpu.VMEM((ff, width), BF16),
            dma((2,)),
            dma((ne,)), dma((ne,)), dma((ne,)), dma((ne,)),
            ring_sems, ring_sems, ring_sems, ring_sems,
            dma((ne,)), dma((ne,)),
            dma, dma,
            ring_sems, ring_sems,
            dma((ne,)), dma((ne,)),
            dma((nf,)), dma((nf,)),
            dma((6,)),
        ],
        compiler_params=pltpu.CompilerParams(
            collective_id=0, has_side_effects=True, vmem_limit_bytes=62 * 1024 * 1024
        ),
    )(
        tokens, cotangent, expert_ids.T, gate_values.T,
        w_in.reshape(width, ff), w_out.reshape(ff, width),
    )
    return (
        out[0],
        out[1].T,
        out[2].reshape(w_in.shape),
        out[3].reshape(w_out.shape),
    )


def solution(mesh):
    return jax.shard_map(
        functools.partial(local, mesh.shape["fsdp"], mesh.shape["expert"]),
        mesh=mesh,
        in_specs=(
            P("expert", None),
            P("expert", None),
            P("expert", None),
            P("expert", None),
            P(None, "expert", "fsdp"),
            P("fsdp", "expert", None),
        ),
        out_specs=(
            P("expert", None),
            P("expert", None),
            P(None, "expert", "fsdp"),
            P("fsdp", "expert", None),
        ),
        check_vma=False,
    )
```

```python
import functools

import jax
import jax.numpy as jnp
from jax import lax
from jax.experimental import pallas as pl
from jax.experimental.pallas import tpu as pltpu
from jax.sharding import PartitionSpec as P

CAP = 40
F32 = jnp.float32
BF16 = jnp.bfloat16
MESH = pl.DeviceIdType.MESH
LANE = 128
PIECES = 4


def nt(a, b):
    return lax.dot_general(a, b, (((1,), (1,)), ((), ())), preferred_element_type=F32)


def tn(a, b):
    return lax.dot_general(a, b, (((0,), (0,)), ((), ())), preferred_element_type=F32)


def flat(v):
    return v.astype(F32).reshape(v.shape[0] * v.shape[1], v.shape[2]).astype(BF16)


def blocks(v):
    return v.reshape(v.shape[0] // CAP, CAP, v.shape[1])


def kernel(
    nf, ne, tok_ref, cot_ref, ids_ref, gates_ref, win_hbm, wout_hbm,
    out_ref, ogate_ref, gin_hbm, gout_hbm,
    win, wout, sel32, sel, x2, g2, send_x, x_all, send_g, g_all, pre, gp16, ag16,
    rs_send, rs_recv, back_send, back_recv, pair_send, pair_recv, tok_all,
    gs_send, gs_recv, gf_all, gin, gout,
    load_sem, x_ss, x_rs, g_ss, g_rs, xr_ss, xr_rs, rs_ss, rs_rs, bk_ss, bk_rs,
    pr_ss, pr_rs, tr_ss, tr_rs, gs_ss, gs_rs, gf_ss, gf_rs, fw_ss, fw_rs, st_sem,
):
    me_f, me_e = lax.axis_index("fsdp"), lax.axis_index("expert")
    nz = nf // 2
    lo, z = me_f // nz, me_f % nz
    rows, width = tok_ref.shape
    wz = width // nz
    ff = win.shape[1]
    top = ids_ref.shape[0]
    slots = ne * CAP
    he, hs = ne // 2, slots // 2
    pair_f = (1 - lo) * nz + z
    wl = width // LANE // 3 * LANE
    wn = width - wl
    wm = wn + LANE
    right_f = lo * nz + (z + 1) % nz
    left_f = lo * nz + (z + nz - 1) % nz

    def dev(f, e):
        return {"fsdp": f, "expert": e}

    def remote(src, dst, ss, rs, f, e):
        return pltpu.make_async_remote_copy(
            src_ref=src, dst_ref=dst, send_sem=ss, recv_sem=rs,
            device_id=dev(f, e), device_id_type=MESH,
        )

    def near(e):
        return (lo + (e // 2) % 2 + (me_e // 2) % 2) % 2

    def near_f(e):
        return near(e) * nz + z

    barrier = pltpu.get_barrier_semaphore()

    def greet_e(k, c):
        e = (me_e + k) % ne
        pl.semaphore_signal(barrier, inc=1, device_id=dev(near_f(e), e), device_id_type=MESH)
        return c

    def greet_f(k, c):
        pl.semaphore_signal(barrier, inc=1, device_id=dev((me_f + k) % nf, me_e), device_id_type=MESH)
        return c

    lax.fori_loop(1, ne, greet_e, 0)
    lax.fori_loop(1, nf, greet_f, 0)
    load_in = pltpu.make_async_copy(win_hbm, win, load_sem.at[0])
    load_out = pltpu.make_async_copy(wout_hbm, wout, load_sem.at[1])
    load_in.start()
    load_out.start()

    ids = ids_ref[...]
    gates = gates_ref[...].astype(F32)
    exps = lax.broadcasted_iota(jnp.int32, (ne, rows), 0)
    named = jnp.zeros((ne, rows), F32)
    gate_of = jnp.zeros((ne, rows), F32)
    for k in range(top):
        hit = exps == ids[k : k + 1, :]
        named = named + jnp.where(hit, 1.0, 0.0)
        gate_of = gate_of + jnp.where(hit, gates[k : k + 1, :], 0.0)
    before = lax.broadcasted_iota(jnp.int32, (rows, rows), 0) < lax.broadcasted_iota(
        jnp.int32, (rows, rows), 1
    )
    place = jnp.dot(
        named.astype(BF16), jnp.where(before, 1.0, 0.0).astype(BF16), preferred_element_type=F32
    )
    place = jnp.where(named > 0.5, place, -1.0)
    slot_no = lax.broadcasted_iota(jnp.int32, (CAP, rows), 0).astype(F32)
    for e in range(ne):
        one = jnp.where(slot_no == place[e : e + 1, :], 1.0, 0.0)
        sel32[e] = one
        gate_col = jnp.sum(one * gate_of[e : e + 1, :], axis=1, keepdims=True)
        send_g[e, :, wn : wn + LANE] = jnp.broadcast_to(gate_col, (CAP, LANE)).astype(BF16)
    sel[...] = sel32[...].reshape(slots, rows).astype(BF16)
    pick = sel[...]
    cols = pl.ds(pl.multiple_of(z * wz, LANE), wz)
    send_x[...] = blocks(jnp.dot(pick, tok_ref[:, cols], preferred_element_type=F32)).astype(BF16)

    pl.semaphore_wait(barrier, (ne - 1) + (nf - 1))

    def x_copy(k):
        e = (me_e + k) % ne
        return remote(send_x.at[e], x_all.at[z, me_e], x_ss.at[e], x_rs.at[me_e], near_f(e), e)

    def x_start(k, c):
        x_copy(k).start()
        return c

    lax.fori_loop(1, ne, x_start, 0)
    own_x = pltpu.make_async_copy(send_x.at[me_e], x_all.at[z, me_e], st_sem.at[0])
    own_x.start()

    gw = 4 * LANE if wl % (4 * LANE) == 0 and wn % (4 * LANE) == 0 else LANE

    def g_build(j, c):
        src = pl.ds(pl.multiple_of(j * gw, LANE), gw)
        dst = pl.ds(pl.multiple_of(j * gw + j // (wn // gw) * LANE, LANE), gw)
        send_g[:, :, dst] = blocks(
            jnp.dot(sel[...], cot_ref[:, src], preferred_element_type=F32)
        ).astype(BF16)
        return c

    lax.fori_loop(0, width // gw, g_build, 0)

    def g_part(side):
        return pl.ds(pl.multiple_of(side * wl, LANE), wm)

    def g_copy(e):
        part = g_part(near(e))
        return remote(
            send_g.at[e, :, part], g_all.at[me_e, :, part], g_ss.at[e], g_rs.at[me_e], near_f(e), e
        )

    def g_arrival(b):
        part = g_part(lo)
        return remote(
            send_g.at[b, :, part], g_all.at[b, :, part], g_ss.at[b], g_rs.at[b], near_f(b), b
        )

    def fw_copy(b, side):
        part = pl.ds(pl.multiple_of(side * wm, LANE), wl)
        ref = g_all.at[b, :, part]
        return remote(ref, ref, fw_ss.at[b], fw_rs.at[b], pair_f, me_e)

    def g_start(k, c):
        g_copy((me_e + k) % ne).start()
        return c

    lax.fori_loop(1, ne, g_start, 0)
    own_g = pltpu.make_async_copy(send_g.at[me_e], g_all.at[me_e], st_sem.at[1])
    own_g.start()

    def x_wait(k, c):
        b = (me_e + ne - k) % ne
        remote(send_x.at[b], x_all.at[z, b], x_ss.at[b], x_rs.at[b], near_f(b), b).wait_recv()
        return c

    lax.fori_loop(1, ne, x_wait, 0)
    own_x.wait()

    far = nz // 2

    def hops(direction, h):
        return far if direction == h else far - 1

    def ring_copy(buf, lead, ss, rs, direction, h, i):
        piece = (z + nz - i) % nz if direction == 0 else (z + i) % nz
        ref = lead(buf, piece, h)
        return remote(
            ref, ref, ss.at[direction, h, i], rs.at[direction, h, i],
            right_f if direction == 0 else left_f, me_e,
        )

    def ring_arrival(buf, lead, ss, rs, direction, h, i):
        piece = (z + nz - 1 - i) % nz if direction == 0 else (z + 1 + i) % nz
        ref = lead(buf, piece, h)
        return remote(
            ref, ref, ss.at[direction, h, i], rs.at[direction, h, i],
            right_f if direction == 0 else left_f, me_e,
        )

    def ring(buf, lead, ss, rs, between):
        for i in range(far + 1):
            for h in (0, 1):
                for d in (0, 1):
                    if 0 < i <= hops(d, h):
                        ring_arrival(buf, lead, ss, rs, d, h, i - 1).wait_recv()
                    if i < hops(d, h):
                        ring_copy(buf, lead, ss, rs, d, h, i).start()
            between(i)

    def ring_drain(buf, lead, ss, rs):
        for i in range(far):
            for h in (0, 1):
                for d in (0, 1):
                    if i < hops(d, h):
                        ring_copy(buf, lead, ss, rs, d, h, i).wait_send()

    def x_lead(buf, piece, h):
        return buf.at[piece, pl.ds(h * he, he)]

    def add_pre(c):
        w_rows = win[pl.ds(pl.multiple_of(c * wz, LANE), wz), :]
        for h in (0, 1):
            xs = flat(x_all[c, h * he : (h + 1) * he])
            x2[c, h * hs : (h + 1) * hs, :] = xs
            pre[h * hs : (h + 1) * hs, :] += jnp.dot(xs, w_rows, preferred_element_type=F32)

    pre[...] = jnp.zeros_like(pre)

    order = list(range(1, ne))
    if ne == 16:
        order = [1, 2, 3, 4, 12, 5, 13, 6, 14, 7, 15, 8, 9, 10, 11]

    def forward(i):
        n = len(order)
        for k in order[n * i // (far + 1) : n * (i + 1) // (far + 1)]:
            b = (me_e + ne - k) % ne
            g_arrival(b).wait_recv()
            fw_copy(b, lo).start()

    def x_between(i):
        forward(i)
        if i == 0:
            load_in.wait()
            add_pre(z)
            return
        add_pre((z + nz - i) % nz)
        if i < far:
            add_pre((z + i) % nz)

    ring(x_all, x_lead, xr_ss, xr_rs, x_between)

    def g_flat(p):
        at = pl.ds(pl.multiple_of(p * 2 * CAP, 16), 2 * CAP)
        two = pl.ds(2 * p, 2)
        g2[at, :wn] = flat(g_all[two, :, :wn])
        g2[at, wn:] = flat(g_all[two, :, wn + LANE :])

    own_g.wait()
    fw_copy(me_e + 1 - 2 * (me_e % 2), 1 - lo).wait_recv()
    g_flat(me_e // 2)

    def g_take(k, c):
        p = (me_e // 2 + he - k) % he
        fw_copy(2 * p, 1 - lo).wait_recv()
        fw_copy(2 * p + 1, 1 - lo).wait_recv()
        g_flat(p)
        return c

    lax.fori_loop(1, he, g_take, 0)
    load_out.wait()

    for h in (0, 1):
        span = slice(h * hs, (h + 1) * hs)
        up = nt(g2[span, :], wout[...])
        gate = g_all[h * he : (h + 1) * he, :, wn : wn + LANE].astype(F32).reshape(hs, LANE)
        gate = jnp.concatenate([gate] * (ff // LANE), axis=1)
        p = pre[span, :]
        squash = jax.nn.sigmoid(p)
        active = p * squash
        part = jnp.sum(active * up, axis=1, keepdims=True)
        gs_send[h * he : (h + 1) * he] = blocks(jnp.broadcast_to(part, (hs, LANE)))
        ag16[span, :] = (gate * active).astype(BF16)
        gp16[span, :] = (gate * squash * (1.0 + p * (1.0 - squash)) * up).astype(BF16)

    def share(c, h):
        return blocks(
            nt(gp16[h * hs : (h + 1) * hs, :], win[pl.ds(pl.multiple_of(c * wz, LANE), wz), :])
        )

    def rs_src(d, h, i):
        return rs_send.at[d, h] if i == 0 else rs_recv.at[d, h, i - 1]

    def rs_copy(d, h, i):
        return remote(
            rs_src(d, h, i), rs_recv.at[d, h, i], rs_ss.at[d, h, i], rs_rs.at[d, h, i],
            right_f if d == 0 else left_f, me_e,
        )

    def rs_step(d, h, i):
        n = hops(d, h)
        c = (z + n - i) % nz if d == 0 else (z + nz - (n - i)) % nz
        total = share(c, h)
        if i > 0:
            rs_copy(d, h, i - 1).wait_recv()
            total = total + rs_src(d, h, i)[...].astype(F32)
        rs_src(d, h, i)[...] = total.astype(BF16)
        rs_copy(d, h, i).start()

    def gs_start(k, c):
        e = (me_e + k) % ne
        remote(gs_send.at[e], gs_recv.at[me_e], gs_ss.at[e], gs_rs.at[me_e], near_f(e), e).start()
        return c

    def gs_wait(k, c):
        b = (me_e + ne - k) % ne
        remote(gs_send.at[b], gs_recv.at[b], gs_ss.at[b], gs_rs.at[b], near_f(b), b).wait_recv()
        return c

    def grad_in_piece(c):
        gin[pl.ds(pl.multiple_of(c * wz, LANE), wz), :] = tn(
            x2[c], gp16[...]
        ).astype(BF16)

    def grad_out_piece(c):
        span = pl.ds(pl.multiple_of(c * wz, LANE), wz)
        gout[:, span] = tn(
            ag16[...], g2[:, span]
        ).astype(BF16)

    def grads(first, last):
        def one(c, carry):
            grad_in_piece(c)
            grad_out_piece(c)
            return carry

        lax.fori_loop(first, last, one, 0)

    def gates_pass():
        lax.fori_loop(1, ne, gs_wait, 0)
        own_gs.wait()
        acc = jnp.zeros((top, rows), F32)
        for e in range(ne):
            row = jnp.sum(sel32[e] * gs_recv[e], axis=0, keepdims=True)
            acc = acc + jnp.where(ids_ref[...] == e, row, 0.0)
        gf_all[me_f, :top, :] = acc

        def gf_start(k, c):
            f = (me_f + k) % nf
            remote(gf_all.at[me_f], gf_all.at[me_f], gf_ss.at[f], gf_rs.at[me_f], f, me_e).start()
            return c

        lax.fori_loop(1, nf, gf_start, 0)

    own_gs = pltpu.make_async_copy(gs_send.at[me_e], gs_recv.at[me_e], st_sem.at[2])
    for i in range(far):
        for h in (0, 1):
            for d in (0, 1):
                if i < hops(d, h):
                    rs_step(d, h, i)
        if i == 0:
            lax.fori_loop(1, ne, gs_start, 0)
            own_gs.start()
        grads(i * nz // far, (i + 1) * nz // far)
        if i == 0:
            gates_pass()
    store_in = pltpu.make_async_copy(gin, gin_hbm, st_sem.at[3])
    store_out = pltpu.make_async_copy(gout, gout_hbm, st_sem.at[4])
    store_in.start()
    store_out.start()

    def back_start(k, c):
        e = (me_e + k) % ne
        remote(back_send.at[e], back_recv.at[me_e], bk_ss.at[e], bk_rs.at[me_e], near_f(e), e).start()
        return c

    def back_wait(k, c):
        b = (me_e + ne - k) % ne
        remote(back_send.at[b], back_recv.at[b], bk_ss.at[b], bk_rs.at[b], near_f(b), b).wait_recv()
        return c

    for h in (0, 1):
        total = share(z, h)
        for d in (0, 1):
            last = hops(d, h) - 1
            rs_copy(d, h, last).wait_recv()
            total = total + rs_recv[d, h, last].astype(F32)
        back_send[h * he : (h + 1) * he] = total.astype(BF16)
    lax.fori_loop(1, ne, back_start, 0)
    own_back = pltpu.make_async_copy(back_send.at[me_e], back_recv.at[me_e], st_sem.at[5])
    own_back.start()

    def gf_wait(k, c):
        f = (me_f + nf - k) % nf
        remote(gf_all.at[f], gf_all.at[f], gf_ss.at[f], gf_rs.at[f], f, me_e).wait_recv()
        return c

    lax.fori_loop(1, nf, gf_wait, 0)
    total_gate = gf_all[0, :top, :]
    for f in range(1, nf):
        total_gate = total_gate + gf_all[f, :top, :]
    ogate_ref[...] = total_gate.astype(BF16)

    lax.fori_loop(1, ne, back_wait, 0)
    own_back.wait()
    tok = tn(sel[...], flat(back_recv[...]))
    pair_send[...] = tok
    pair = remote(pair_send, pair_recv, pr_ss, pr_rs, pair_f, me_e)
    pair.start()
    pair.wait_recv()
    tok_all[z] = (pair_send[...] + pair_recv[...]).astype(BF16)

    hr = rows // 2

    def t_lead(buf, piece, h):
        return buf.at[piece, pl.ds(h * hr, hr)]

    ring(tok_all, t_lead, tr_ss, tr_rs, lambda i: None)
    for c in range(nz):
        out_ref[:, c * wz : (c + 1) * wz] = tok_all[c]

    def drain(k, c):
        e = (me_e + k) % ne
        x_copy(k).wait_send()
        g_copy(e).wait_send()
        fw_copy(e, lo).wait_send()
        remote(gs_send.at[e], gs_recv.at[me_e], gs_ss.at[e], gs_rs.at[me_e], near_f(e), e).wait_send()
        remote(back_send.at[e], back_recv.at[me_e], bk_ss.at[e], bk_rs.at[me_e], near_f(e), e).wait_send()
        return c

    def drain_f(k, c):
        f = (me_f + k) % nf
        remote(gf_all.at[me_f], gf_all.at[me_f], gf_ss.at[f], gf_rs.at[me_f], f, me_e).wait_send()
        return c

    lax.fori_loop(1, ne, drain, 0)
    lax.fori_loop(1, nf, drain_f, 0)
    ring_drain(x_all, x_lead, xr_ss, xr_rs)
    ring_drain(tok_all, t_lead, tr_ss, tr_rs)
    for i in range(far):
        for h in (0, 1):
            for d in (0, 1):
                if i < hops(d, h):
                    rs_copy(d, h, i).wait_send()
    pair.wait_send()
    store_in.wait()
    store_out.wait()


def passing(a0, a1, a2, a3, o0, o1, o2, o3, b0, b1, b2, b3, sems):
    moves = []
    for n, (a, o, b) in enumerate(((a0, o0, b0), (a1, o1, b1), (a2, o2, b2), (a3, o3, b3))):
        pieces = PIECES if n > 1 else 1
        step = a.shape[0] // pieces
        for p in range(pieces):
            at = pl.ds(p * step, step)
            moves.append((
                pltpu.make_async_copy(a.at[at], b.at[at], sems.at[0, n, p]),
                pltpu.make_async_copy(b.at[at], o.at[at], sems.at[1, n, p]),
            ))
    for get, _ in moves:
        get.start()
    for get, put in moves:
        get.wait()
        put.start()
    for _, put in moves:
        put.wait()


def local(nf, ne, tokens, cotangent, expert_ids, gate_values, w_in, w_out):
    rows, width = tokens.shape
    top = expert_ids.shape[1]
    ff = w_in.shape[2]
    nz = nf // 2
    wz = width // nz
    far = nz // 2
    he = ne // 2
    dma = pltpu.SemaphoreType.DMA
    vmem = pl.BlockSpec(memory_space=pltpu.VMEM)
    hbm = pl.BlockSpec(memory_space=pl.ANY)
    ring_sems = dma((2, 2, far))
    out = pl.pallas_call(
        functools.partial(kernel, nf, ne),
        out_shape=(
            jax.ShapeDtypeStruct((rows, width), BF16),
            jax.ShapeDtypeStruct((top, rows), BF16),
            jax.ShapeDtypeStruct((width, ff), BF16),
            jax.ShapeDtypeStruct((ff, width), BF16),
        ),
        in_specs=[vmem, vmem, vmem, vmem, hbm, hbm],
        out_specs=(vmem, vmem, hbm, hbm),
        scratch_shapes=[
            pltpu.VMEM((width, ff), BF16),
            pltpu.VMEM((ff, width), BF16),
            pltpu.VMEM((ne, CAP, rows), F32),
            pltpu.VMEM((ne * CAP, rows), BF16),
            pltpu.VMEM((nz, ne * CAP, wz), BF16),
            pltpu.VMEM((ne * CAP, width), BF16),
            pltpu.VMEM((ne, CAP, wz), BF16),
            pltpu.VMEM((nz, ne, CAP, wz), BF16),
            pltpu.VMEM((ne, CAP, width + LANE), BF16),
            pltpu.VMEM((ne, CAP, width + LANE), BF16),
            pltpu.VMEM((ne * CAP, ff), F32),
            pltpu.VMEM((ne * CAP, ff), BF16),
            pltpu.VMEM((ne * CAP, ff), BF16),
            pltpu.VMEM((2, 2, he, CAP, wz), BF16),
            pltpu.VMEM((2, 2, far, he, CAP, wz), BF16),
            pltpu.VMEM((ne, CAP, wz), BF16),
            pltpu.VMEM((ne, CAP, wz), BF16),
            pltpu.VMEM((rows, wz), F32),
            pltpu.VMEM((rows, wz), F32),
            pltpu.VMEM((nz, rows, wz), BF16),
            pltpu.VMEM((ne, CAP, LANE), F32),
            pltpu.VMEM((ne, CAP, LANE), F32),
            pltpu.VMEM((nf, 8, rows), F32),
            pltpu.VMEM((width, ff), BF16),
            pltpu.VMEM((ff, width), BF16),
            dma((2,)),
            dma((ne,)), dma((ne,)), dma((ne,)), dma((ne,)),
            ring_sems, ring_sems, ring_sems, ring_sems,
            dma((ne,)), dma((ne,)),
            dma, dma,
            ring_sems, ring_sems,
            dma((ne,)), dma((ne,)),
            dma((nf,)), dma((nf,)),
            dma((ne,)), dma((ne,)),
            dma((6,)),
        ],
        compiler_params=pltpu.CompilerParams(
            collective_id=0, has_side_effects=True, vmem_limit_bytes=62 * 1024 * 1024
        ),
    )(
        tokens, cotangent, expert_ids.T, gate_values.T,
        w_in.reshape(width, ff), w_out.reshape(ff, width),
    )
    out = pl.pallas_call(
        passing,
        out_shape=tuple(jax.ShapeDtypeStruct(a.shape, a.dtype) for a in out),
        in_specs=[hbm] * 4,
        out_specs=(hbm,) * 4,
        scratch_shapes=[pltpu.VMEM(a.shape, a.dtype) for a in out] + [dma((2, 4, PIECES))],
        compiler_params=pltpu.CompilerParams(vmem_limit_bytes=62 * 1024 * 1024),
    )(*out)
    return (
        out[0],
        out[1].T,
        out[2].reshape(w_in.shape),
        out[3].reshape(w_out.shape),
    )


def solution(mesh):
    return jax.shard_map(
        functools.partial(local, mesh.shape["fsdp"], mesh.shape["expert"]),
        mesh=mesh,
        in_specs=(
            P("expert", None),
            P("expert", None),
            P("expert", None),
            P("expert", None),
            P(None, "expert", "fsdp"),
            P("fsdp", "expert", None),
        ),
        out_specs=(
            P("expert", None),
            P("expert", None),
            P(None, "expert", "fsdp"),
            P("fsdp", "expert", None),
        ),
        check_vma=False,
    )
```

```python
import functools

import jax
import jax.numpy as jnp
from jax import lax
from jax.experimental import pallas as pl
from jax.experimental.pallas import tpu as pltpu
from jax.sharding import PartitionSpec as P

CAP = 40
F32 = jnp.float32
BF16 = jnp.bfloat16
MESH = pl.DeviceIdType.MESH
LANE = 128
PIECES = 4


def nt(a, b):
    return lax.dot_general(a, b, (((1,), (1,)), ((), ())), preferred_element_type=F32)


def tn(a, b):
    return lax.dot_general(a, b, (((0,), (0,)), ((), ())), preferred_element_type=F32)


def flat(v):
    return v.astype(F32).reshape(v.shape[0] * v.shape[1], v.shape[2]).astype(BF16)


def blocks(v):
    return v.reshape(v.shape[0] // CAP, CAP, v.shape[1])


def kernel(
    nf, ne, tok_ref, cot_ref, ids_ref, gates_ref, win_hbm, wout_hbm,
    out_ref, ogate_ref, gin_hbm, gout_hbm,
    win, wout, sel32, sel, x2, g2, send_x, x_all, send_g, g_all, pre, gp16, ag16,
    rs_send, rs_recv, back_send, back_recv, pair_send, pair_recv, tok_all,
    gs_send, gs_recv, gf_all, gin, gout, d_send, d_recv, ts_send, ts_recv,
    load_sem, x_ss, x_rs, g_ss, g_rs, xr_ss, xr_rs, rs_ss, rs_rs, bk_ss, bk_rs,
    pr_ss, pr_rs, tr_ss, tr_rs, gs_ss, gs_rs, gf_ss, gf_rs, d_ss, d_rs, ts_ss, ts_rs, st_sem,
):
    me_f, me_e = lax.axis_index("fsdp"), lax.axis_index("expert")
    nz = nf // 2
    lo, z = me_f // nz, me_f % nz
    rows, width = tok_ref.shape
    wz = width // nz
    ff = win.shape[1]
    top = ids_ref.shape[0]
    slots = ne * CAP
    he, hs = ne // 2, slots // 2
    sub = LANE
    wr = wz - sub
    pair_f = (1 - lo) * nz + z
    right_f = lo * nz + (z + 1) % nz
    left_f = lo * nz + (z + nz - 1) % nz

    def dev(f, e):
        return {"fsdp": f, "expert": e}

    def remote(src, dst, ss, rs, f, e):
        return pltpu.make_async_remote_copy(
            src_ref=src, dst_ref=dst, send_sem=ss, recv_sem=rs,
            device_id=dev(f, e), device_id_type=MESH,
        )

    barrier = pltpu.get_barrier_semaphore()

    def greet_e(k, c):
        pl.semaphore_signal(barrier, inc=1, device_id=dev(me_f, (me_e + k) % ne), device_id_type=MESH)
        return c

    def greet_f(k, c):
        pl.semaphore_signal(barrier, inc=1, device_id=dev((me_f + k) % nf, me_e), device_id_type=MESH)
        return c

    lax.fori_loop(1, ne, greet_e, 0)
    lax.fori_loop(1, nf, greet_f, 0)
    load_in = pltpu.make_async_copy(win_hbm, win, load_sem.at[0])
    load_out = pltpu.make_async_copy(wout_hbm, wout, load_sem.at[1])
    load_in.start()
    load_out.start()

    ids = ids_ref[...]
    gates = gates_ref[...].astype(F32)
    exps = lax.broadcasted_iota(jnp.int32, (ne, rows), 0)
    named = jnp.zeros((ne, rows), F32)
    gate_of = jnp.zeros((ne, rows), F32)
    for k in range(top):
        hit = exps == ids[k : k + 1, :]
        named = named + jnp.where(hit, 1.0, 0.0)
        gate_of = gate_of + jnp.where(hit, gates[k : k + 1, :], 0.0)
    before = lax.broadcasted_iota(jnp.int32, (rows, rows), 0) < lax.broadcasted_iota(
        jnp.int32, (rows, rows), 1
    )
    place = jnp.dot(
        named.astype(BF16), jnp.where(before, 1.0, 0.0).astype(BF16), preferred_element_type=F32
    )
    place = jnp.where(named > 0.5, place, -1.0)
    slot_no = lax.broadcasted_iota(jnp.int32, (CAP, rows), 0).astype(F32)
    for e in range(ne):
        one = jnp.where(slot_no == place[e : e + 1, :], 1.0, 0.0)
        sel32[e] = one
        gate_col = jnp.sum(one * gate_of[e : e + 1, :], axis=1, keepdims=True)
        send_g[e, :, width:] = jnp.broadcast_to(gate_col, (CAP, LANE)).astype(BF16)
    sel[...] = sel32[...].reshape(slots, rows).astype(BF16)
    pick = sel[...]
    cols = pl.ds(pl.multiple_of(z * wz, LANE), wz)
    send_x[...] = blocks(jnp.dot(pick, tok_ref[:, cols], preferred_element_type=F32)).astype(BF16)

    pl.semaphore_wait(barrier, (ne - 1) + (nf - 1))

    def x_copy(k):
        e = (me_e + k) % ne
        return remote(send_x.at[e], x_all.at[z, me_e], x_ss.at[e], x_rs.at[me_e], me_f, e)

    def x_start(k, c):
        x_copy(k).start()
        return c

    lax.fori_loop(1, ne, x_start, 0)
    own_x = pltpu.make_async_copy(send_x.at[me_e], x_all.at[z, me_e], st_sem.at[0])
    own_x.start()

    gw = width // 6 if width % (6 * LANE) == 0 else width

    def g_build(j, c):
        span = pl.ds(pl.multiple_of(j * gw, LANE), gw)
        send_g[:, :, span] = blocks(
            jnp.dot(sel[...], cot_ref[:, span], preferred_element_type=F32)
        ).astype(BF16)
        return c

    lax.fori_loop(0, width // gw, g_build, 0)

    def g_start(k, c):
        e = (me_e + k) % ne
        remote(send_g.at[e], g_all.at[me_e], g_ss.at[e], g_rs.at[me_e], me_f, e).start()
        return c

    lax.fori_loop(1, ne, g_start, 0)
    own_g = pltpu.make_async_copy(send_g.at[me_e], g_all.at[me_e], st_sem.at[1])
    own_g.start()

    def x_wait(k, c):
        b = (me_e + ne - k) % ne
        remote(send_x.at[b], x_all.at[z, b], x_ss.at[b], x_rs.at[b], me_f, b).wait_recv()
        return c

    lax.fori_loop(1, ne, x_wait, 0)
    own_x.wait()

    far = nz // 2

    def hops(direction, h):
        return far if direction == h else far - 1

    def ring_copy(buf, lead, ss, rs, direction, h, i):
        piece = (z + nz - i) % nz if direction == 0 else (z + i) % nz
        ref = lead(buf, piece, h)
        return remote(
            ref, ref, ss.at[direction, h, i], rs.at[direction, h, i],
            right_f if direction == 0 else left_f, me_e,
        )

    def ring_arrival(buf, lead, ss, rs, direction, h, i):
        piece = (z + nz - 1 - i) % nz if direction == 0 else (z + 1 + i) % nz
        ref = lead(buf, piece, h)
        return remote(
            ref, ref, ss.at[direction, h, i], rs.at[direction, h, i],
            right_f if direction == 0 else left_f, me_e,
        )

    def ring(buf, lead, ss, rs, between):
        for i in range(far + 1):
            for h in (0, 1):
                for d in (0, 1):
                    if 0 < i <= hops(d, h):
                        ring_arrival(buf, lead, ss, rs, d, h, i - 1).wait_recv()
                    if i < hops(d, h):
                        ring_copy(buf, lead, ss, rs, d, h, i).start()
            between(i)

    def ring_drain(buf, lead, ss, rs):
        for i in range(far):
            for h in (0, 1):
                for d in (0, 1):
                    if i < hops(d, h):
                        ring_copy(buf, lead, ss, rs, d, h, i).wait_send()

    def x_lead(buf, piece, h):
        return buf.at[piece, pl.ds(h * he, he)]

    def add_pre(c):
        w_rows = win[pl.ds(pl.multiple_of(c * wz, LANE), wz), :]
        for h in (0, 1):
            xs = flat(x_all[c, h * he : (h + 1) * he])
            x2[c, h * hs : (h + 1) * hs, :] = xs
            pre[h * hs : (h + 1) * hs, :] += jnp.dot(xs, w_rows, preferred_element_type=F32)

    pre[...] = jnp.zeros_like(pre)

    def x_between(i):
        if i == 0:
            load_in.wait()
            add_pre(z)
            return
        add_pre((z + nz - i) % nz)
        if i < far:
            add_pre((z + i) % nz)

    ring(x_all, x_lead, xr_ss, xr_rs, x_between)

    def g_arrival(b):
        return remote(send_g.at[b], g_all.at[b], g_ss.at[b], g_rs.at[b], me_f, b)

    def g_flat(p):
        g2[pl.ds(pl.multiple_of(p * 2 * CAP, 16), 2 * CAP), :] = flat(
            g_all[pl.ds(2 * p, 2), :, :width]
        )

    own_g.wait()
    g_arrival(me_e + 1 - 2 * (me_e % 2)).wait_recv()
    g_flat(me_e // 2)

    def g_take(k, c):
        p = (me_e // 2 + he - k) % he
        g_arrival(2 * p).wait_recv()
        g_arrival(2 * p + 1).wait_recv()
        g_flat(p)
        return c

    lax.fori_loop(1, he, g_take, 0)
    load_out.wait()

    for h in (0, 1):
        span = slice(h * hs, (h + 1) * hs)
        up = nt(g2[span, :], wout[...])
        gate = g_all[h * he : (h + 1) * he, :, width:].astype(F32).reshape(hs, LANE)
        gate = jnp.concatenate([gate] * (ff // LANE), axis=1)
        p = pre[span, :]
        squash = jax.nn.sigmoid(p)
        active = p * squash
        part = jnp.sum(active * up, axis=1, keepdims=True)
        gs_send[h * he : (h + 1) * he] = blocks(jnp.broadcast_to(part, (hs, LANE)))
        ag16[span, :] = (gate * active).astype(BF16)
        gp16[span, :] = (gate * squash * (1.0 + p * (1.0 - squash)) * up).astype(BF16)

    def share(c, h):
        part = win[pl.ds(pl.multiple_of(c * wz + sub, LANE), wr), :]
        return blocks(nt(gp16[h * hs : (h + 1) * hs, :], part))

    def direct_build(c, carry):
        part = win[pl.ds(pl.multiple_of(c * wz, LANE), sub), :]
        d_send[:, :, pl.ds(pl.multiple_of(c * sub, LANE), sub)] = blocks(
            nt(gp16[...], part)
        ).astype(BF16)
        return carry

    def d_start(k, c):
        e = (me_e + k) % ne
        remote(d_send.at[e], d_recv.at[me_e], d_ss.at[e], d_rs.at[me_e], me_f, e).start()
        return c

    def d_wait(k, c):
        b = (me_e + ne - k) % ne
        remote(d_send.at[b], d_recv.at[b], d_ss.at[b], d_rs.at[b], me_f, b).wait_recv()
        return c

    def t_start(k, c):
        o = (z + k) % nz
        remote(
            ts_send.at[o], ts_recv.at[z], ts_ss.at[o], ts_rs.at[z], lo * nz + o, me_e
        ).start()
        return c

    def t_wait(k, c):
        o = (z + nz - k) % nz
        remote(
            ts_send.at[o], ts_recv.at[o], ts_ss.at[o], ts_rs.at[o], lo * nz + o, me_e
        ).wait_recv()
        return c

    def direct_combine():
        lax.fori_loop(1, ne, d_wait, 0)
        own_d.wait()

        def one(c, carry):
            part = flat(d_recv[:, :, pl.ds(pl.multiple_of(c * sub, LANE), sub)])
            ts_send[c] = tn(sel[...], part).astype(BF16)
            return carry

        lax.fori_loop(0, nz, one, 0)
        lax.fori_loop(1, nz, t_start, 0)

    own_d = pltpu.make_async_copy(d_send.at[me_e], d_recv.at[me_e], st_sem.at[6])

    def rs_src(d, h, i):
        return rs_send.at[d, h] if i == 0 else rs_recv.at[d, h, i - 1]

    def rs_copy(d, h, i):
        return remote(
            rs_src(d, h, i), rs_recv.at[d, h, i], rs_ss.at[d, h, i], rs_rs.at[d, h, i],
            right_f if d == 0 else left_f, me_e,
        )

    def rs_step(d, h, i):
        n = hops(d, h)
        c = (z + n - i) % nz if d == 0 else (z + nz - (n - i)) % nz
        total = share(c, h)
        if i > 0:
            rs_copy(d, h, i - 1).wait_recv()
            total = total + rs_src(d, h, i)[...].astype(F32)
        rs_src(d, h, i)[...] = total.astype(BF16)
        rs_copy(d, h, i).start()

    def gs_start(k, c):
        e = (me_e + k) % ne
        remote(gs_send.at[e], gs_recv.at[me_e], gs_ss.at[e], gs_rs.at[me_e], me_f, e).start()
        return c

    def gs_wait(k, c):
        b = (me_e + ne - k) % ne
        remote(gs_send.at[b], gs_recv.at[b], gs_ss.at[b], gs_rs.at[b], me_f, b).wait_recv()
        return c

    def grad_in_piece(c):
        gin[pl.ds(pl.multiple_of(c * wz, LANE), wz), :] = tn(
            x2[c], gp16[...]
        ).astype(BF16)

    def grad_out_piece(c):
        span = pl.ds(pl.multiple_of(c * wz, LANE), wz)
        gout[:, span] = tn(
            ag16[...], g2[:, span]
        ).astype(BF16)

    def grads(first, last):
        def one(c, carry):
            grad_in_piece(c)
            grad_out_piece(c)
            return carry

        lax.fori_loop(first, last, one, 0)

    def gates_pass():
        lax.fori_loop(1, ne, gs_wait, 0)
        own_gs.wait()
        acc = jnp.zeros((top, rows), F32)
        for e in range(ne):
            row = jnp.sum(sel32[e] * gs_recv[e], axis=0, keepdims=True)
            acc = acc + jnp.where(ids_ref[...] == e, row, 0.0)
        gf_all[me_f, :top, :] = acc

        def gf_start(k, c):
            f = (me_f + k) % nf
            remote(gf_all.at[me_f], gf_all.at[me_f], gf_ss.at[f], gf_rs.at[me_f], f, me_e).start()
            return c

        lax.fori_loop(1, nf, gf_start, 0)

    own_gs = pltpu.make_async_copy(gs_send.at[me_e], gs_recv.at[me_e], st_sem.at[2])
    for i in range(far):
        for h in (0, 1):
            for d in (0, 1):
                if i < hops(d, h):
                    rs_step(d, h, i)
        if i == 0:
            lax.fori_loop(1, ne, gs_start, 0)
            own_gs.start()
            lax.fori_loop(0, nz, direct_build, 0)
            lax.fori_loop(1, ne, d_start, 0)
            own_d.start()
        grads(i * nz // far, (i + 1) * nz // far)
        if i == 0:
            gates_pass()
        if i == max(far - 2, 0):
            direct_combine()
    store_in = pltpu.make_async_copy(gin, gin_hbm, st_sem.at[3])
    store_out = pltpu.make_async_copy(gout, gout_hbm, st_sem.at[4])
    store_in.start()
    store_out.start()

    def back_start(k, c):
        e = (me_e + k) % ne
        remote(back_send.at[e], back_recv.at[me_e], bk_ss.at[e], bk_rs.at[me_e], me_f, e).start()
        return c

    def back_wait(k, c):
        b = (me_e + ne - k) % ne
        remote(back_send.at[b], back_recv.at[b], bk_ss.at[b], bk_rs.at[b], me_f, b).wait_recv()
        return c

    for h in (0, 1):
        total = share(z, h)
        for d in (0, 1):
            last = hops(d, h) - 1
            rs_copy(d, h, last).wait_recv()
            total = total + rs_recv[d, h, last].astype(F32)
        back_send[h * he : (h + 1) * he] = total.astype(BF16)
    lax.fori_loop(1, ne, back_start, 0)
    own_back = pltpu.make_async_copy(back_send.at[me_e], back_recv.at[me_e], st_sem.at[5])
    own_back.start()

    def gf_wait(k, c):
        f = (me_f + nf - k) % nf
        remote(gf_all.at[f], gf_all.at[f], gf_ss.at[f], gf_rs.at[f], f, me_e).wait_recv()
        return c

    lax.fori_loop(1, nf, gf_wait, 0)
    total_gate = gf_all[0, :top, :]
    for f in range(1, nf):
        total_gate = total_gate + gf_all[f, :top, :]
    ogate_ref[...] = total_gate.astype(BF16)

    lax.fori_loop(1, nz, t_wait, 0)
    total = ts_send[z].astype(F32)
    for k in range(1, nz):
        total = total + ts_recv[(z + k) % nz].astype(F32)
    pair_send[:, :sub] = total

    lax.fori_loop(1, ne, back_wait, 0)
    own_back.wait()
    tok = tn(sel[...], flat(back_recv[...]))
    pair_send[:, sub:] = tok
    pair = remote(pair_send, pair_recv, pr_ss, pr_rs, pair_f, me_e)
    pair.start()
    pair.wait_recv()
    tok_all[z] = (pair_send[...] + pair_recv[...]).astype(BF16)

    hr = rows // 2

    def t_lead(buf, piece, h):
        return buf.at[piece, pl.ds(h * hr, hr)]

    ring(tok_all, t_lead, tr_ss, tr_rs, lambda i: None)
    for c in range(nz):
        out_ref[:, c * wz : (c + 1) * wz] = tok_all[c]

    def drain(k, c):
        e = (me_e + k) % ne
        remote(send_x.at[e], x_all.at[z, me_e], x_ss.at[e], x_rs.at[me_e], me_f, e).wait_send()
        remote(send_g.at[e], g_all.at[me_e], g_ss.at[e], g_rs.at[me_e], me_f, e).wait_send()
        remote(gs_send.at[e], gs_recv.at[me_e], gs_ss.at[e], gs_rs.at[me_e], me_f, e).wait_send()
        remote(d_send.at[e], d_recv.at[me_e], d_ss.at[e], d_rs.at[me_e], me_f, e).wait_send()
        remote(back_send.at[e], back_recv.at[me_e], bk_ss.at[e], bk_rs.at[me_e], me_f, e).wait_send()
        return c

    def drain_f(k, c):
        f = (me_f + k) % nf
        remote(gf_all.at[me_f], gf_all.at[me_f], gf_ss.at[f], gf_rs.at[me_f], f, me_e).wait_send()
        return c

    lax.fori_loop(1, ne, drain, 0)
    lax.fori_loop(1, nf, drain_f, 0)

    def drain_z(k, c):
        o = (z + k) % nz
        remote(
            ts_send.at[o], ts_recv.at[z], ts_ss.at[o], ts_rs.at[z], lo * nz + o, me_e
        ).wait_send()
        return c

    lax.fori_loop(1, nz, drain_z, 0)
    ring_drain(x_all, x_lead, xr_ss, xr_rs)
    ring_drain(tok_all, t_lead, tr_ss, tr_rs)
    for i in range(far):
        for h in (0, 1):
            for d in (0, 1):
                if i < hops(d, h):
                    rs_copy(d, h, i).wait_send()
    pair.wait_send()
    store_in.wait()
    store_out.wait()


def passing(a0, a1, a2, a3, o0, o1, o2, o3, b0, b1, b2, b3, sems):
    moves = []
    for n, (a, o, b) in enumerate(((a0, o0, b0), (a1, o1, b1), (a2, o2, b2), (a3, o3, b3))):
        pieces = PIECES if n > 1 else 1
        step = a.shape[0] // pieces
        for p in range(pieces):
            at = pl.ds(p * step, step)
            moves.append((
                pltpu.make_async_copy(a.at[at], b.at[at], sems.at[0, n, p]),
                pltpu.make_async_copy(b.at[at], o.at[at], sems.at[1, n, p]),
            ))
    for get, _ in moves:
        get.start()
    for get, put in moves:
        get.wait()
        put.start()
    for _, put in moves:
        put.wait()


def local(nf, ne, tokens, cotangent, expert_ids, gate_values, w_in, w_out):
    rows, width = tokens.shape
    top = expert_ids.shape[1]
    ff = w_in.shape[2]
    nz = nf // 2
    wz = width // nz
    far = nz // 2
    he = ne // 2
    dma = pltpu.SemaphoreType.DMA
    vmem = pl.BlockSpec(memory_space=pltpu.VMEM)
    hbm = pl.BlockSpec(memory_space=pl.ANY)
    ring_sems = dma((2, 2, far))
    out = pl.pallas_call(
        functools.partial(kernel, nf, ne),
        out_shape=(
            jax.ShapeDtypeStruct((rows, width), BF16),
            jax.ShapeDtypeStruct((top, rows), BF16),
            jax.ShapeDtypeStruct((width, ff), BF16),
            jax.ShapeDtypeStruct((ff, width), BF16),
        ),
        in_specs=[vmem, vmem, vmem, vmem, hbm, hbm],
        out_specs=(vmem, vmem, hbm, hbm),
        scratch_shapes=[
            pltpu.VMEM((width, ff), BF16),
            pltpu.VMEM((ff, width), BF16),
            pltpu.VMEM((ne, CAP, rows), F32),
            pltpu.VMEM((ne * CAP, rows), BF16),
            pltpu.VMEM((nz, ne * CAP, wz), BF16),
            pltpu.VMEM((ne * CAP, width), BF16),
            pltpu.VMEM((ne, CAP, wz), BF16),
            pltpu.VMEM((nz, ne, CAP, wz), BF16),
            pltpu.VMEM((ne, CAP, width + LANE), BF16),
            pltpu.VMEM((ne, CAP, width + LANE), BF16),
            pltpu.VMEM((ne * CAP, ff), F32),
            pltpu.VMEM((ne * CAP, ff), BF16),
            pltpu.VMEM((ne * CAP, ff), BF16),
            pltpu.VMEM((2, 2, he, CAP, wz - LANE), BF16),
            pltpu.VMEM((2, 2, far, he, CAP, wz - LANE), BF16),
            pltpu.VMEM((ne, CAP, wz - LANE), BF16),
            pltpu.VMEM((ne, CAP, wz - LANE), BF16),
            pltpu.VMEM((rows, wz), F32),
            pltpu.VMEM((rows, wz), F32),
            pltpu.VMEM((nz, rows, wz), BF16),
            pltpu.VMEM((ne, CAP, LANE), F32),
            pltpu.VMEM((ne, CAP, LANE), F32),
            pltpu.VMEM((nf, 8, rows), F32),
            pltpu.VMEM((width, ff), BF16),
            pltpu.VMEM((ff, width), BF16),
            pltpu.VMEM((ne, CAP, nz * LANE), BF16),
            pltpu.VMEM((ne, CAP, nz * LANE), BF16),
            pltpu.VMEM((nz, rows, LANE), BF16),
            pltpu.VMEM((nz, rows, LANE), BF16),
            dma((2,)),
            dma((ne,)), dma((ne,)), dma((ne,)), dma((ne,)),
            ring_sems, ring_sems, ring_sems, ring_sems,
            dma((ne,)), dma((ne,)),
            dma, dma,
            ring_sems, ring_sems,
            dma((ne,)), dma((ne,)),
            dma((nf,)), dma((nf,)),
            dma((ne,)), dma((ne,)), dma((nz,)), dma((nz,)),
            dma((7,)),
        ],
        compiler_params=pltpu.CompilerParams(
            collective_id=0, has_side_effects=True, vmem_limit_bytes=62 * 1024 * 1024
        ),
    )(
        tokens, cotangent, expert_ids.T, gate_values.T,
        w_in.reshape(width, ff), w_out.reshape(ff, width),
    )
    out = pl.pallas_call(
        passing,
        out_shape=tuple(jax.ShapeDtypeStruct(a.shape, a.dtype) for a in out),
        in_specs=[hbm] * 4,
        out_specs=(hbm,) * 4,
        scratch_shapes=[pltpu.VMEM(a.shape, a.dtype) for a in out] + [dma((2, 4, PIECES))],
        compiler_params=pltpu.CompilerParams(vmem_limit_bytes=62 * 1024 * 1024),
    )(*out)
    return (
        out[0],
        out[1].T,
        out[2].reshape(w_in.shape),
        out[3].reshape(w_out.shape),
    )


def solution(mesh):
    return jax.shard_map(
        functools.partial(local, mesh.shape["fsdp"], mesh.shape["expert"]),
        mesh=mesh,
        in_specs=(
            P("expert", None),
            P("expert", None),
            P("expert", None),
            P("expert", None),
            P(None, "expert", "fsdp"),
            P("fsdp", "expert", None),
        ),
        out_specs=(
            P("expert", None),
            P("expert", None),
            P(None, "expert", "fsdp"),
            P("fsdp", "expert", None),
        ),
        check_vma=False,
    )
```

```python
import functools

import jax
import jax.numpy as jnp
from jax import lax
from jax.experimental import pallas as pl
from jax.experimental.pallas import tpu as pltpu
from jax.sharding import PartitionSpec as P

CAP = 40
F32 = jnp.float32
BF16 = jnp.bfloat16
MESH = pl.DeviceIdType.MESH
LANE = 128
PIECES = 4


def nt(a, b):
    return lax.dot_general(a, b, (((1,), (1,)), ((), ())), preferred_element_type=F32)


def tn(a, b):
    return lax.dot_general(a, b, (((0,), (0,)), ((), ())), preferred_element_type=F32)


def flat(v):
    return v.astype(F32).reshape(v.shape[0] * v.shape[1], v.shape[2]).astype(BF16)


def blocks(v):
    return v.reshape(v.shape[0] // CAP, CAP, v.shape[1])


def kernel(
    nf, ne, tok_ref, cot_ref, ids_ref, gates_ref, win_hbm, wout_hbm,
    out_ref, ogate_ref, gin_hbm, gout_hbm,
    win, wout, sel32, sel, x2, g2, send_x, x_all, send_g, g_all, pre, gp16, ag16,
    rs_send, rs_recv, back_send, back_recv, pair_send, pair_recv, tok_all,
    gs_send, gs_recv, gf_all, gin, gout, d_send, d_recv, ts_send, ts_recv,
    load_sem, x_ss, x_rs, g_ss, g_rs, xr_ss, xr_rs, rs_ss, rs_rs, bk_ss, bk_rs,
    pr_ss, pr_rs, tr_ss, tr_rs, gs_ss, gs_rs, gf_ss, gf_rs, d_ss, d_rs, ts_ss, ts_rs, st_sem,
):
    me_f, me_e = lax.axis_index("fsdp"), lax.axis_index("expert")
    nz = nf // 2
    lo, z = me_f // nz, me_f % nz
    rows, width = tok_ref.shape
    wz = width // nz
    ff = win.shape[1]
    top = ids_ref.shape[0]
    slots = ne * CAP
    he, hs = ne // 2, slots // 2
    sub = LANE
    wr = wz - sub
    pair_f = (1 - lo) * nz + z
    right_f = lo * nz + (z + 1) % nz
    left_f = lo * nz + (z + nz - 1) % nz

    def dev(f, e):
        return {"fsdp": f, "expert": e}

    def remote(src, dst, ss, rs, f, e):
        return pltpu.make_async_remote_copy(
            src_ref=src, dst_ref=dst, send_sem=ss, recv_sem=rs,
            device_id=dev(f, e), device_id_type=MESH,
        )

    barrier = pltpu.get_barrier_semaphore()

    def greet_e(k, c):
        pl.semaphore_signal(barrier, inc=1, device_id=dev(me_f, (me_e + k) % ne), device_id_type=MESH)
        return c

    def greet_f(k, c):
        pl.semaphore_signal(barrier, inc=1, device_id=dev((me_f + k) % nf, me_e), device_id_type=MESH)
        return c

    lax.fori_loop(1, ne, greet_e, 0)
    lax.fori_loop(1, nf, greet_f, 0)
    load_in = pltpu.make_async_copy(win_hbm, win, load_sem.at[0])
    load_out = pltpu.make_async_copy(wout_hbm, wout, load_sem.at[1])
    load_in.start()
    load_out.start()

    ids = ids_ref[...]
    gates = gates_ref[...].astype(F32)
    exps = lax.broadcasted_iota(jnp.int32, (ne, rows), 0)
    named = jnp.zeros((ne, rows), F32)
    gate_of = jnp.zeros((ne, rows), F32)
    for k in range(top):
        hit = exps == ids[k : k + 1, :]
        named = named + jnp.where(hit, 1.0, 0.0)
        gate_of = gate_of + jnp.where(hit, gates[k : k + 1, :], 0.0)
    before = lax.broadcasted_iota(jnp.int32, (rows, rows), 0) < lax.broadcasted_iota(
        jnp.int32, (rows, rows), 1
    )
    place = jnp.dot(
        named.astype(BF16), jnp.where(before, 1.0, 0.0).astype(BF16), preferred_element_type=F32
    )
    place = jnp.where(named > 0.5, place, -1.0)
    slot_no = lax.broadcasted_iota(jnp.int32, (CAP, rows), 0).astype(F32)
    for e in range(ne):
        one = jnp.where(slot_no == place[e : e + 1, :], 1.0, 0.0)
        sel32[e] = one
        gate_col = jnp.sum(one * gate_of[e : e + 1, :], axis=1, keepdims=True)
        send_g[e, :, width:] = jnp.broadcast_to(gate_col, (CAP, LANE)).astype(BF16)
    sel[...] = sel32[...].reshape(slots, rows).astype(BF16)
    pick = sel[...]
    cols = pl.ds(pl.multiple_of(z * wz, LANE), wz)
    send_x[...] = blocks(jnp.dot(pick, tok_ref[:, cols], preferred_element_type=F32)).astype(BF16)

    pl.semaphore_wait(barrier, (ne - 1) + (nf - 1))

    def x_copy(k):
        e = (me_e + k) % ne
        return remote(send_x.at[e], x_all.at[z, me_e], x_ss.at[e], x_rs.at[me_e], me_f, e)

    def x_start(k, c):
        x_copy(k).start()
        return c

    lax.fori_loop(1, ne, x_start, 0)
    own_x = pltpu.make_async_copy(send_x.at[me_e], x_all.at[z, me_e], st_sem.at[0])
    own_x.start()

    gw = width // 6 if width % (6 * LANE) == 0 else width

    def g_build(j, c):
        span = pl.ds(pl.multiple_of(j * gw, LANE), gw)
        send_g[:, :, span] = blocks(
            jnp.dot(sel[...], cot_ref[:, span], preferred_element_type=F32)
        ).astype(BF16)
        return c

    lax.fori_loop(0, width // gw, g_build, 0)

    def g_start(k, c):
        e = (me_e + k) % ne
        remote(send_g.at[e], g_all.at[me_e], g_ss.at[e], g_rs.at[me_e], me_f, e).start()
        return c

    lax.fori_loop(1, ne, g_start, 0)
    own_g = pltpu.make_async_copy(send_g.at[me_e], g_all.at[me_e], st_sem.at[1])
    own_g.start()

    def x_wait(k, c):
        b = (me_e + ne - k) % ne
        remote(send_x.at[b], x_all.at[z, b], x_ss.at[b], x_rs.at[b], me_f, b).wait_recv()
        return c

    lax.fori_loop(1, ne, x_wait, 0)
    own_x.wait()

    far = nz // 2

    def hops(direction, h):
        return far if direction == h else far - 1

    def ring_copy(buf, lead, ss, rs, direction, h, i):
        piece = (z + nz - i) % nz if direction == 0 else (z + i) % nz
        ref = lead(buf, piece, h)
        return remote(
            ref, ref, ss.at[direction, h, i], rs.at[direction, h, i],
            right_f if direction == 0 else left_f, me_e,
        )

    def ring_arrival(buf, lead, ss, rs, direction, h, i):
        piece = (z + nz - 1 - i) % nz if direction == 0 else (z + 1 + i) % nz
        ref = lead(buf, piece, h)
        return remote(
            ref, ref, ss.at[direction, h, i], rs.at[direction, h, i],
            right_f if direction == 0 else left_f, me_e,
        )

    def ring(buf, lead, ss, rs, between):
        for i in range(far + 1):
            for h in (0, 1):
                for d in (0, 1):
                    if 0 < i <= hops(d, h):
                        ring_arrival(buf, lead, ss, rs, d, h, i - 1).wait_recv()
                    if i < hops(d, h):
                        ring_copy(buf, lead, ss, rs, d, h, i).start()
            between(i)

    def ring_drain(buf, lead, ss, rs):
        for i in range(far):
            for h in (0, 1):
                for d in (0, 1):
                    if i < hops(d, h):
                        ring_copy(buf, lead, ss, rs, d, h, i).wait_send()

    def x_lead(buf, piece, h):
        return buf.at[piece, pl.ds(h * he, he)]

    def add_pre(c):
        w_rows = win[pl.ds(pl.multiple_of(c * wz, LANE), wz), :]
        for h in (0, 1):
            xs = flat(x_all[c, h * he : (h + 1) * he])
            x2[c, h * hs : (h + 1) * hs, :] = xs
            pre[h * hs : (h + 1) * hs, :] += jnp.dot(xs, w_rows, preferred_element_type=F32)

    pre[...] = jnp.zeros_like(pre)

    def x_between(i):
        if i == 0:
            load_in.wait()
            add_pre(z)
            return
        add_pre((z + nz - i) % nz)
        if i < far:
            add_pre((z + i) % nz)

    ring(x_all, x_lead, xr_ss, xr_rs, x_between)

    def g_arrival(b):
        return remote(send_g.at[b], g_all.at[b], g_ss.at[b], g_rs.at[b], me_f, b)

    def g_flat(p):
        g2[pl.ds(pl.multiple_of(p * 2 * CAP, 16), 2 * CAP), :] = flat(
            g_all[pl.ds(2 * p, 2), :, :width]
        )

    own_g.wait()
    g_arrival(me_e + 1 - 2 * (me_e % 2)).wait_recv()
    g_flat(me_e // 2)

    def g_take(k, c):
        p = (me_e // 2 + he - k) % he
        g_arrival(2 * p).wait_recv()
        g_arrival(2 * p + 1).wait_recv()
        g_flat(p)
        return c

    lax.fori_loop(1, he, g_take, 0)
    load_out.wait()

    for h in (0, 1):
        span = slice(h * hs, (h + 1) * hs)
        up = nt(g2[span, :], wout[...])
        gate = g_all[h * he : (h + 1) * he, :, width:].astype(F32).reshape(hs, LANE)
        gate = jnp.concatenate([gate] * (ff // LANE), axis=1)
        p = pre[span, :]
        squash = jax.nn.sigmoid(p)
        active = p * squash
        part = jnp.sum(active * up, axis=1, keepdims=True)
        gs_send[h * he : (h + 1) * he] = blocks(jnp.broadcast_to(part, (hs, LANE)))
        ag16[span, :] = (gate * active).astype(BF16)
        gp16[span, :] = (gate * squash * (1.0 + p * (1.0 - squash)) * up).astype(BF16)

    def share(c, h):
        part = win[pl.ds(pl.multiple_of(c * wz + sub, LANE), wr), :]
        return blocks(nt(gp16[h * hs : (h + 1) * hs, :], part))

    def direct_build(c, carry):
        part = win[pl.ds(pl.multiple_of(c * wz, LANE), sub), :]
        d_send[:, :, pl.ds(pl.multiple_of(c * sub, LANE), sub)] = blocks(
            nt(gp16[...], part)
        ).astype(BF16)
        return carry

    def d_start(k, c):
        e = (me_e + k) % ne
        remote(d_send.at[e], d_recv.at[me_e], d_ss.at[e], d_rs.at[me_e], me_f, e).start()
        return c

    def d_wait(k, c):
        b = (me_e + ne - k) % ne
        remote(d_send.at[b], d_recv.at[b], d_ss.at[b], d_rs.at[b], me_f, b).wait_recv()
        return c

    def t_start(k, c):
        o = (z + k) % nz
        remote(
            ts_send.at[o], ts_recv.at[z], ts_ss.at[o], ts_rs.at[z], lo * nz + o, me_e
        ).start()
        return c

    def t_wait(k, c):
        o = (z + nz - k) % nz
        remote(
            ts_send.at[o], ts_recv.at[o], ts_ss.at[o], ts_rs.at[o], lo * nz + o, me_e
        ).wait_recv()
        return c

    def direct_combine():
        lax.fori_loop(1, ne, d_wait, 0)
        own_d.wait()

        def one(c, carry):
            part = flat(d_recv[:, :, pl.ds(pl.multiple_of(c * sub, LANE), sub)])
            ts_send[c] = tn(sel[...], part).astype(BF16)
            return carry

        lax.fori_loop(0, nz, one, 0)
        lax.fori_loop(1, nz, t_start, 0)

    own_d = pltpu.make_async_copy(d_send.at[me_e], d_recv.at[me_e], st_sem.at[6])

    def rs_src(d, h, i):
        return rs_send.at[d, h] if i == 0 else rs_recv.at[d, h, i - 1]

    def rs_copy(d, h, i):
        return remote(
            rs_src(d, h, i), rs_recv.at[d, h, i], rs_ss.at[d, h, i], rs_rs.at[d, h, i],
            right_f if d == 0 else left_f, me_e,
        )

    def rs_step(d, h, i):
        n = hops(d, h)
        c = (z + n - i) % nz if d == 0 else (z + nz - (n - i)) % nz
        total = share(c, h)
        if i > 0:
            rs_copy(d, h, i - 1).wait_recv()
            total = total + rs_src(d, h, i)[...].astype(F32)
        rs_src(d, h, i)[...] = total.astype(BF16)
        rs_copy(d, h, i).start()

    def gs_start(k, c):
        e = (me_e + k) % ne
        remote(gs_send.at[e], gs_recv.at[me_e], gs_ss.at[e], gs_rs.at[me_e], me_f, e).start()
        return c

    def gs_wait(k, c):
        b = (me_e + ne - k) % ne
        remote(gs_send.at[b], gs_recv.at[b], gs_ss.at[b], gs_rs.at[b], me_f, b).wait_recv()
        return c

    def grad_in_piece(c):
        gin[pl.ds(pl.multiple_of(c * wz, LANE), wz), :] = tn(
            x2[c], gp16[...]
        ).astype(BF16)

    def grad_out_piece(c):
        span = pl.ds(pl.multiple_of(c * wz, LANE), wz)
        gout[:, span] = tn(
            ag16[...], g2[:, span]
        ).astype(BF16)

    def grads(first, last):
        def one(c, carry):
            grad_in_piece(c)
            grad_out_piece(c)
            return carry

        lax.fori_loop(first, last, one, 0)

    def gates_pass():
        lax.fori_loop(1, ne, gs_wait, 0)
        own_gs.wait()
        acc = jnp.zeros((top, rows), F32)
        for e in range(ne):
            row = jnp.sum(sel32[e] * gs_recv[e], axis=0, keepdims=True)
            acc = acc + jnp.where(ids_ref[...] == e, row, 0.0)
        gf_all[me_f, :top, :] = acc

        def gf_start(k, c):
            f = (me_f + k) % nf
            remote(gf_all.at[me_f], gf_all.at[me_f], gf_ss.at[f], gf_rs.at[me_f], f, me_e).start()
            return c

        lax.fori_loop(1, nf, gf_start, 0)

    own_gs = pltpu.make_async_copy(gs_send.at[me_e], gs_recv.at[me_e], st_sem.at[2])
    for i in range(far):
        for h in (0, 1):
            for d in (0, 1):
                if i < hops(d, h):
                    rs_step(d, h, i)
        if i == 0:
            lax.fori_loop(1, ne, gs_start, 0)
            own_gs.start()
            lax.fori_loop(0, nz, direct_build, 0)
            lax.fori_loop(1, ne, d_start, 0)
            own_d.start()
        grads(i * nz // far, (i + 1) * nz // far)
        if i == far - 1:
            gates_pass()
            direct_combine()
    store_in = pltpu.make_async_copy(gin, gin_hbm, st_sem.at[3])
    store_out = pltpu.make_async_copy(gout, gout_hbm, st_sem.at[4])
    store_in.start()
    store_out.start()

    def back_start(k, c):
        e = (me_e + k) % ne
        remote(back_send.at[e], back_recv.at[me_e], bk_ss.at[e], bk_rs.at[me_e], me_f, e).start()
        return c

    def back_wait(k, c):
        b = (me_e + ne - k) % ne
        remote(back_send.at[b], back_recv.at[b], bk_ss.at[b], bk_rs.at[b], me_f, b).wait_recv()
        return c

    for h in (0, 1):
        total = share(z, h)
        for d in (0, 1):
            last = hops(d, h) - 1
            rs_copy(d, h, last).wait_recv()
            total = total + rs_recv[d, h, last].astype(F32)
        back_send[h * he : (h + 1) * he] = total.astype(BF16)
    lax.fori_loop(1, ne, back_start, 0)
    own_back = pltpu.make_async_copy(back_send.at[me_e], back_recv.at[me_e], st_sem.at[5])
    own_back.start()

    def gf_wait(k, c):
        f = (me_f + nf - k) % nf
        remote(gf_all.at[f], gf_all.at[f], gf_ss.at[f], gf_rs.at[f], f, me_e).wait_recv()
        return c

    lax.fori_loop(1, nf, gf_wait, 0)
    total_gate = gf_all[0, :top, :]
    for f in range(1, nf):
        total_gate = total_gate + gf_all[f, :top, :]
    ogate_ref[...] = total_gate.astype(BF16)

    lax.fori_loop(1, nz, t_wait, 0)
    total = ts_send[z].astype(F32)
    for k in range(1, nz):
        total = total + ts_recv[(z + k) % nz].astype(F32)
    pair_send[:, :sub] = total

    lax.fori_loop(1, ne, back_wait, 0)
    own_back.wait()
    tok = tn(sel[...], flat(back_recv[...]))
    pair_send[:, sub:] = tok
    pair = remote(pair_send, pair_recv, pr_ss, pr_rs, pair_f, me_e)
    pair.start()
    pair.wait_recv()
    tok_all[z] = (pair_send[...] + pair_recv[...]).astype(BF16)

    hr = rows // 2

    def t_lead(buf, piece, h):
        return buf.at[piece, pl.ds(h * hr, hr)]

    ring(tok_all, t_lead, tr_ss, tr_rs, lambda i: None)
    for c in range(nz):
        out_ref[:, c * wz : (c + 1) * wz] = tok_all[c]

    def drain(k, c):
        e = (me_e + k) % ne
        remote(send_x.at[e], x_all.at[z, me_e], x_ss.at[e], x_rs.at[me_e], me_f, e).wait_send()
        remote(send_g.at[e], g_all.at[me_e], g_ss.at[e], g_rs.at[me_e], me_f, e).wait_send()
        remote(gs_send.at[e], gs_recv.at[me_e], gs_ss.at[e], gs_rs.at[me_e], me_f, e).wait_send()
        remote(d_send.at[e], d_recv.at[me_e], d_ss.at[e], d_rs.at[me_e], me_f, e).wait_send()
        remote(back_send.at[e], back_recv.at[me_e], bk_ss.at[e], bk_rs.at[me_e], me_f, e).wait_send()
        return c

    def drain_f(k, c):
        f = (me_f + k) % nf
        remote(gf_all.at[me_f], gf_all.at[me_f], gf_ss.at[f], gf_rs.at[me_f], f, me_e).wait_send()
        return c

    lax.fori_loop(1, ne, drain, 0)
    lax.fori_loop(1, nf, drain_f, 0)

    def drain_z(k, c):
        o = (z + k) % nz
        remote(
            ts_send.at[o], ts_recv.at[z], ts_ss.at[o], ts_rs.at[z], lo * nz + o, me_e
        ).wait_send()
        return c

    lax.fori_loop(1, nz, drain_z, 0)
    ring_drain(x_all, x_lead, xr_ss, xr_rs)
    ring_drain(tok_all, t_lead, tr_ss, tr_rs)
    for i in range(far):
        for h in (0, 1):
            for d in (0, 1):
                if i < hops(d, h):
                    rs_copy(d, h, i).wait_send()
    pair.wait_send()
    store_in.wait()
    store_out.wait()


def passing(a0, a1, a2, a3, o0, o1, o2, o3, b0, b1, b2, b3, sems):
    moves = []
    for n, (a, o, b) in enumerate(((a0, o0, b0), (a1, o1, b1), (a2, o2, b2), (a3, o3, b3))):
        pieces = PIECES if n > 1 else 1
        step = a.shape[0] // pieces
        for p in range(pieces):
            at = pl.ds(p * step, step)
            moves.append((
                pltpu.make_async_copy(a.at[at], b.at[at], sems.at[0, n, p]),
                pltpu.make_async_copy(b.at[at], o.at[at], sems.at[1, n, p]),
            ))
    for get, _ in moves:
        get.start()
    for get, put in moves:
        get.wait()
        put.start()
    for _, put in moves:
        put.wait()


def local(nf, ne, tokens, cotangent, expert_ids, gate_values, w_in, w_out):
    rows, width = tokens.shape
    top = expert_ids.shape[1]
    ff = w_in.shape[2]
    nz = nf // 2
    wz = width // nz
    far = nz // 2
    he = ne // 2
    dma = pltpu.SemaphoreType.DMA
    vmem = pl.BlockSpec(memory_space=pltpu.VMEM)
    hbm = pl.BlockSpec(memory_space=pl.ANY)
    ring_sems = dma((2, 2, far))
    out = pl.pallas_call(
        functools.partial(kernel, nf, ne),
        out_shape=(
            jax.ShapeDtypeStruct((rows, width), BF16),
            jax.ShapeDtypeStruct((top, rows), BF16),
            jax.ShapeDtypeStruct((width, ff), BF16),
            jax.ShapeDtypeStruct((ff, width), BF16),
        ),
        in_specs=[vmem, vmem, vmem, vmem, hbm, hbm],
        out_specs=(vmem, vmem, hbm, hbm),
        scratch_shapes=[
            pltpu.VMEM((width, ff), BF16),
            pltpu.VMEM((ff, width), BF16),
            pltpu.VMEM((ne, CAP, rows), F32),
            pltpu.VMEM((ne * CAP, rows), BF16),
            pltpu.VMEM((nz, ne * CAP, wz), BF16),
            pltpu.VMEM((ne * CAP, width), BF16),
            pltpu.VMEM((ne, CAP, wz), BF16),
            pltpu.VMEM((nz, ne, CAP, wz), BF16),
            pltpu.VMEM((ne, CAP, width + LANE), BF16),
            pltpu.VMEM((ne, CAP, width + LANE), BF16),
            pltpu.VMEM((ne * CAP, ff), F32),
            pltpu.VMEM((ne * CAP, ff), BF16),
            pltpu.VMEM((ne * CAP, ff), BF16),
            pltpu.VMEM((2, 2, he, CAP, wz - LANE), BF16),
            pltpu.VMEM((2, 2, far, he, CAP, wz - LANE), BF16),
            pltpu.VMEM((ne, CAP, wz - LANE), BF16),
            pltpu.VMEM((ne, CAP, wz - LANE), BF16),
            pltpu.VMEM((rows, wz), F32),
            pltpu.VMEM((rows, wz), F32),
            pltpu.VMEM((nz, rows, wz), BF16),
            pltpu.VMEM((ne, CAP, LANE), F32),
            pltpu.VMEM((ne, CAP, LANE), F32),
            pltpu.VMEM((nf, 8, rows), F32),
            pltpu.VMEM((width, ff), BF16),
            pltpu.VMEM((ff, width), BF16),
            pltpu.VMEM((ne, CAP, nz * LANE), BF16),
            pltpu.VMEM((ne, CAP, nz * LANE), BF16),
            pltpu.VMEM((nz, rows, LANE), BF16),
            pltpu.VMEM((nz, rows, LANE), BF16),
            dma((2,)),
            dma((ne,)), dma((ne,)), dma((ne,)), dma((ne,)),
            ring_sems, ring_sems, ring_sems, ring_sems,
            dma((ne,)), dma((ne,)),
            dma, dma,
            ring_sems, ring_sems,
            dma((ne,)), dma((ne,)),
            dma((nf,)), dma((nf,)),
            dma((ne,)), dma((ne,)), dma((nz,)), dma((nz,)),
            dma((7,)),
        ],
        compiler_params=pltpu.CompilerParams(
            collective_id=0, has_side_effects=True, vmem_limit_bytes=62 * 1024 * 1024
        ),
    )(
        tokens, cotangent, expert_ids.T, gate_values.T,
        w_in.reshape(width, ff), w_out.reshape(ff, width),
    )
    out = pl.pallas_call(
        passing,
        out_shape=tuple(jax.ShapeDtypeStruct(a.shape, a.dtype) for a in out),
        in_specs=[hbm] * 4,
        out_specs=(hbm,) * 4,
        scratch_shapes=[pltpu.VMEM(a.shape, a.dtype) for a in out] + [dma((2, 4, PIECES))],
        compiler_params=pltpu.CompilerParams(vmem_limit_bytes=62 * 1024 * 1024),
    )(*out)
    return (
        out[0],
        out[1].T,
        out[2].reshape(w_in.shape),
        out[3].reshape(w_out.shape),
    )


def solution(mesh):
    return jax.shard_map(
        functools.partial(local, mesh.shape["fsdp"], mesh.shape["expert"]),
        mesh=mesh,
        in_specs=(
            P("expert", None),
            P("expert", None),
            P("expert", None),
            P("expert", None),
            P(None, "expert", "fsdp"),
            P("fsdp", "expert", None),
        ),
        out_specs=(
            P("expert", None),
            P("expert", None),
            P(None, "expert", "fsdp"),
            P("fsdp", "expert", None),
        ),
        check_vma=False,
    )
```

```python
import functools

import jax
import jax.numpy as jnp
from jax import lax
from jax.experimental import pallas as pl
from jax.experimental.pallas import tpu as pltpu
from jax.sharding import PartitionSpec as P

CAP = 40
F32 = jnp.float32
BF16 = jnp.bfloat16
MESH = pl.DeviceIdType.MESH
LANE = 128
PIECES = 4


def nt(a, b):
    return lax.dot_general(a, b, (((1,), (1,)), ((), ())), preferred_element_type=F32)


def tn(a, b):
    return lax.dot_general(a, b, (((0,), (0,)), ((), ())), preferred_element_type=F32)


def flat(v):
    return v.astype(F32).reshape(v.shape[0] * v.shape[1], v.shape[2]).astype(BF16)


def blocks(v):
    return v.reshape(v.shape[0] // CAP, CAP, v.shape[1])


def kernel(
    nf, ne, tok_ref, cot_ref, ids_ref, gates_ref, win_hbm, wout_hbm,
    out_ref, ogate_ref, gin_hbm, gout_hbm,
    win, wout, sel32, sel, x2, g2, send_x, x_all, send_g, g_all, pre, gp16, ag16,
    rs_send, rs_recv, back_send, back_recv, pair_send, pair_recv, tok_all,
    gs_send, gs_recv, gf_all, gin, gout, d_send, d_recv, ts_send, ts_recv,
    load_sem, x_ss, x_rs, g_ss, g_rs, xr_ss, xr_rs, rs_ss, rs_rs, bk_ss, bk_rs,
    pr_ss, pr_rs, tr_ss, tr_rs, gs_ss, gs_rs, gf_ss, gf_rs, d_ss, d_rs, ts_ss, ts_rs, sw_ss, sw_rs, st_sem,
):
    me_f, me_e = lax.axis_index("fsdp"), lax.axis_index("expert")
    nz = nf // 2
    lo, z = me_f // nz, me_f % nz
    rows, width = tok_ref.shape
    wz = width // nz
    ff = win.shape[1]
    top = ids_ref.shape[0]
    slots = ne * CAP
    he, hs = ne // 2, slots // 2
    sub = LANE
    wr = wz - sub
    pair_f = (1 - lo) * nz + z
    wg = nz * LANE
    wd = width - wg
    right_f = lo * nz + (z + 1) % nz
    left_f = lo * nz + (z + nz - 1) % nz

    def dev(f, e):
        return {"fsdp": f, "expert": e}

    def remote(src, dst, ss, rs, f, e):
        return pltpu.make_async_remote_copy(
            src_ref=src, dst_ref=dst, send_sem=ss, recv_sem=rs,
            device_id=dev(f, e), device_id_type=MESH,
        )

    def near(e):
        return (lo + (e // 2) % 2 + (me_e // 2) % 2) % 2

    def near_f(e):
        return near(e) * nz + z

    barrier = pltpu.get_barrier_semaphore()

    def greet_e(k, c):
        e = (me_e + k) % ne
        pl.semaphore_signal(barrier, inc=1, device_id=dev(me_f, e), device_id_type=MESH)

        @pl.when(near(e) != lo)
        def _():
            pl.semaphore_signal(barrier, inc=1, device_id=dev(near_f(e), e), device_id_type=MESH)

        return c

    def greet_f(k, c):
        pl.semaphore_signal(barrier, inc=1, device_id=dev((me_f + k) % nf, me_e), device_id_type=MESH)
        return c

    lax.fori_loop(1, ne, greet_e, 0)
    lax.fori_loop(1, nf, greet_f, 0)
    load_in = pltpu.make_async_copy(win_hbm, win, load_sem.at[0])
    load_out = pltpu.make_async_copy(wout_hbm, wout, load_sem.at[1])
    load_in.start()
    load_out.start()

    ids = ids_ref[...]
    gates = gates_ref[...].astype(F32)
    exps = lax.broadcasted_iota(jnp.int32, (ne, rows), 0)
    named = jnp.zeros((ne, rows), F32)
    gate_of = jnp.zeros((ne, rows), F32)
    for k in range(top):
        hit = exps == ids[k : k + 1, :]
        named = named + jnp.where(hit, 1.0, 0.0)
        gate_of = gate_of + jnp.where(hit, gates[k : k + 1, :], 0.0)
    before = lax.broadcasted_iota(jnp.int32, (rows, rows), 0) < lax.broadcasted_iota(
        jnp.int32, (rows, rows), 1
    )
    place = jnp.dot(
        named.astype(BF16), jnp.where(before, 1.0, 0.0).astype(BF16), preferred_element_type=F32
    )
    place = jnp.where(named > 0.5, place, -1.0)
    slot_no = lax.broadcasted_iota(jnp.int32, (CAP, rows), 0).astype(F32)
    for e in range(ne):
        one = jnp.where(slot_no == place[e : e + 1, :], 1.0, 0.0)
        sel32[e] = one
        gate_col = jnp.sum(one * gate_of[e : e + 1, :], axis=1, keepdims=True)
        send_g[e, :, wd:] = jnp.broadcast_to(gate_col, (CAP, LANE)).astype(BF16)
    sel[...] = sel32[...].reshape(slots, rows).astype(BF16)
    pick = sel[...]
    cols = pl.ds(pl.multiple_of(z * wz, LANE), wz)
    send_x[:, :, :wz] = blocks(
        jnp.dot(pick, tok_ref[:, cols], preferred_element_type=F32)
    ).astype(BF16)
    gcol = pl.ds(pl.multiple_of(z * LANE, LANE), LANE)
    send_x[:, :, wz:] = blocks(
        jnp.dot(pick, cot_ref[:, gcol], preferred_element_type=F32)
    ).astype(BF16)

    pl.semaphore_wait(barrier, (ne - 1) + (nf - 1) + ne // 2)

    def side(l):
        return pl.ds(pl.multiple_of(l * LANE, LANE), wz)

    def x_copy(k):
        e = (me_e + k) % ne
        c = side(near(e))
        return remote(
            send_x.at[e, :, c], x_all.at[z, me_e, :, c], x_ss.at[e], x_rs.at[me_e], near_f(e), e
        )

    def x_start(k, c):
        x_copy(k).start()
        return c

    lax.fori_loop(1, ne, x_start, 0)
    own_x = pltpu.make_async_copy(
        send_x.at[me_e, :, side(lo)], x_all.at[z, me_e, :, side(lo)], st_sem.at[0]
    )
    own_x.start()

    gw = 4 * LANE

    def g_build(j, c):
        src = pl.ds(pl.multiple_of(wg + j * gw, LANE), gw)
        send_g[:, :, pl.ds(pl.multiple_of(j * gw, LANE), gw)] = blocks(
            jnp.dot(sel[...], cot_ref[:, src], preferred_element_type=F32)
        ).astype(BF16)
        return c

    lax.fori_loop(0, wd // gw, g_build, 0)

    def g_start(k, c):
        e = (me_e + k) % ne
        remote(send_g.at[e], g_all.at[me_e], g_ss.at[e], g_rs.at[me_e], near_f(e), e).start()
        return c

    lax.fori_loop(1, ne, g_start, 0)
    own_g = pltpu.make_async_copy(send_g.at[me_e], g_all.at[me_e], st_sem.at[1])
    own_g.start()

    def x_wait(k, c):
        b = (me_e + ne - k) % ne
        c2 = side(lo)
        remote(
            send_x.at[b, :, c2], x_all.at[z, b, :, c2], x_ss.at[b], x_rs.at[b], near_f(b), b
        ).wait_recv()
        return c

    lax.fori_loop(1, ne, x_wait, 0)
    own_x.wait()

    far = nz // 2

    def hops(direction, h):
        return far if direction == h else far - 1

    def ring_copy(buf, lead, ss, rs, direction, h, i):
        piece = (z + nz - i) % nz if direction == 0 else (z + i) % nz
        ref = lead(buf, piece, h)
        return remote(
            ref, ref, ss.at[direction, h, i], rs.at[direction, h, i],
            right_f if direction == 0 else left_f, me_e,
        )

    def ring_arrival(buf, lead, ss, rs, direction, h, i):
        piece = (z + nz - 1 - i) % nz if direction == 0 else (z + 1 + i) % nz
        ref = lead(buf, piece, h)
        return remote(
            ref, ref, ss.at[direction, h, i], rs.at[direction, h, i],
            right_f if direction == 0 else left_f, me_e,
        )

    def ring(buf, lead, ss, rs, between, arrived=None):
        for i in range(far + 1):
            for h in (0, 1):
                for d in (0, 1):
                    if 0 < i <= hops(d, h):
                        ring_arrival(buf, lead, ss, rs, d, h, i - 1).wait_recv()
                    if i < hops(d, h):
                        ring_copy(buf, lead, ss, rs, d, h, i).start()
                    if arrived is not None and 0 < i <= hops(d, h):
                        arrived((z + nz - i) % nz if d == 0 else (z + i) % nz, h)
            between(i)

    def ring_drain(buf, lead, ss, rs):
        for i in range(far):
            for h in (0, 1):
                for d in (0, 1):
                    if i < hops(d, h):
                        ring_copy(buf, lead, ss, rs, d, h, i).wait_send()

    def x_lead(buf, piece, h):
        return buf.at[piece, pl.ds(h * he, he), :, side(lo)]

    def swap(c, h, l):
        ref = x_all.at[c, pl.ds(h * he, he), :, pl.ds(pl.multiple_of(l * wz, LANE), LANE)]
        return remote(ref, ref, sw_ss.at[c, h], sw_rs.at[c, h], pair_f, me_e)

    def add_pre(c):
        w_rows = win[pl.ds(pl.multiple_of(c * wz, LANE), wz), :]
        for h in (0, 1):
            swap(c, h, 1 - lo).wait_recv()
            xs = flat(x_all[c, h * he : (h + 1) * he, :, :wz])
            x2[c, h * hs : (h + 1) * hs, :] = xs
            g2[h * hs : (h + 1) * hs, pl.ds(pl.multiple_of(c * LANE, LANE), LANE)] = flat(
                x_all[c, h * he : (h + 1) * he, :, wz:]
            )
            pre[h * hs : (h + 1) * hs, :] += jnp.dot(xs, w_rows, preferred_element_type=F32)

    pre[...] = jnp.zeros_like(pre)

    def x_between(i):
        if i == 0:
            load_in.wait()
        elif i == 1:
            add_pre(z)
        else:
            add_pre((z + nz - i + 1) % nz)
            add_pre((z + i - 1) % nz)

    swap(z, 0, lo).start()
    swap(z, 1, lo).start()
    ring(x_all, x_lead, xr_ss, xr_rs, x_between, lambda c, h: swap(c, h, lo).start())
    add_pre((z + far) % nz)

    def g_arrival(b):
        return remote(send_g.at[b], g_all.at[b], g_ss.at[b], g_rs.at[b], near_f(b), b)

    def g_flat(p):
        g2[pl.ds(pl.multiple_of(p * 2 * CAP, 16), 2 * CAP), wg:] = flat(
            g_all[pl.ds(2 * p, 2), :, :wd]
        )

    own_g.wait()
    g_arrival(me_e + 1 - 2 * (me_e % 2)).wait_recv()
    g_flat(me_e // 2)

    def g_take(k, c):
        p = (me_e // 2 + he - k) % he
        g_arrival(2 * p).wait_recv()
        g_arrival(2 * p + 1).wait_recv()
        g_flat(p)
        return c

    lax.fori_loop(1, he, g_take, 0)
    load_out.wait()

    for h in (0, 1):
        span = slice(h * hs, (h + 1) * hs)
        up = nt(g2[span, :], wout[...])
        gate = g_all[h * he : (h + 1) * he, :, wd:].astype(F32).reshape(hs, LANE)
        gate = jnp.concatenate([gate] * (ff // LANE), axis=1)
        p = pre[span, :]
        squash = jax.nn.sigmoid(p)
        active = p * squash
        part = jnp.sum(active * up, axis=1, keepdims=True)
        gs_send[h * he : (h + 1) * he] = blocks(jnp.broadcast_to(part, (hs, LANE)))
        ag16[span, :] = (gate * active).astype(BF16)
        gp16[span, :] = (gate * squash * (1.0 + p * (1.0 - squash)) * up).astype(BF16)

    def share(c, h):
        part = win[pl.ds(pl.multiple_of(c * wz + sub, LANE), wr), :]
        return blocks(nt(gp16[h * hs : (h + 1) * hs, :], part))

    def direct_build(c, carry):
        part = win[pl.ds(pl.multiple_of(c * wz, LANE), sub), :]
        d_send[:, :, pl.ds(pl.multiple_of(c * sub, LANE), sub)] = blocks(
            nt(gp16[...], part)
        ).astype(BF16)
        return carry

    def d_start(k, c):
        e = (me_e + k) % ne
        remote(d_send.at[e], d_recv.at[me_e], d_ss.at[e], d_rs.at[me_e], me_f, e).start()
        return c

    def d_wait(k, c):
        b = (me_e + ne - k) % ne
        remote(d_send.at[b], d_recv.at[b], d_ss.at[b], d_rs.at[b], me_f, b).wait_recv()
        return c

    def t_start(k, c):
        o = (z + k) % nz
        remote(
            ts_send.at[o], ts_recv.at[z], ts_ss.at[o], ts_rs.at[z], lo * nz + o, me_e
        ).start()
        return c

    def t_wait(k, c):
        o = (z + nz - k) % nz
        remote(
            ts_send.at[o], ts_recv.at[o], ts_ss.at[o], ts_rs.at[o], lo * nz + o, me_e
        ).wait_recv()
        return c

    def direct_combine():
        lax.fori_loop(1, ne, d_wait, 0)
        own_d.wait()

        def one(c, carry):
            part = flat(d_recv[:, :, pl.ds(pl.multiple_of(c * sub, LANE), sub)])
            ts_send[c] = tn(sel[...], part).astype(BF16)
            return carry

        lax.fori_loop(0, nz, one, 0)
        lax.fori_loop(1, nz, t_start, 0)

    own_d = pltpu.make_async_copy(d_send.at[me_e], d_recv.at[me_e], st_sem.at[6])

    def rs_src(d, h, i):
        return rs_send.at[d, h] if i == 0 else rs_recv.at[d, h, i - 1]

    def rs_copy(d, h, i):
        return remote(
            rs_src(d, h, i), rs_recv.at[d, h, i], rs_ss.at[d, h, i], rs_rs.at[d, h, i],
            right_f if d == 0 else left_f, me_e,
        )

    def rs_step(d, h, i):
        n = hops(d, h)
        c = (z + n - i) % nz if d == 0 else (z + nz - (n - i)) % nz
        total = share(c, h)
        if i > 0:
            rs_copy(d, h, i - 1).wait_recv()
            total = total + rs_src(d, h, i)[...].astype(F32)
        rs_src(d, h, i)[...] = total.astype(BF16)
        rs_copy(d, h, i).start()

    def gs_start(k, c):
        e = (me_e + k) % ne
        remote(gs_send.at[e], gs_recv.at[me_e], gs_ss.at[e], gs_rs.at[me_e], me_f, e).start()
        return c

    def gs_wait(k, c):
        b = (me_e + ne - k) % ne
        remote(gs_send.at[b], gs_recv.at[b], gs_ss.at[b], gs_rs.at[b], me_f, b).wait_recv()
        return c

    def grad_in_piece(c):
        gin[pl.ds(pl.multiple_of(c * wz, LANE), wz), :] = tn(
            x2[c], gp16[...]
        ).astype(BF16)

    def grad_out_piece(c):
        span = pl.ds(pl.multiple_of(c * wz, LANE), wz)
        gout[:, span] = tn(
            ag16[...], g2[:, span]
        ).astype(BF16)

    def grads(first, last):
        def one(c, carry):
            grad_in_piece(c)
            grad_out_piece(c)
            return carry

        lax.fori_loop(first, last, one, 0)

    def gates_pass():
        lax.fori_loop(1, ne, gs_wait, 0)
        own_gs.wait()
        acc = jnp.zeros((top, rows), F32)
        for e in range(ne):
            row = jnp.sum(sel32[e] * gs_recv[e], axis=0, keepdims=True)
            acc = acc + jnp.where(ids_ref[...] == e, row, 0.0)
        gf_all[me_f, :top, :] = acc

        def gf_start(k, c):
            f = (me_f + k) % nf
            remote(gf_all.at[me_f], gf_all.at[me_f], gf_ss.at[f], gf_rs.at[me_f], f, me_e).start()
            return c

        lax.fori_loop(1, nf, gf_start, 0)

    own_gs = pltpu.make_async_copy(gs_send.at[me_e], gs_recv.at[me_e], st_sem.at[2])
    for i in range(far):
        for h in (0, 1):
            for d in (0, 1):
                if i < hops(d, h):
                    rs_step(d, h, i)
        if i == 0:
            lax.fori_loop(1, ne, gs_start, 0)
            own_gs.start()
            lax.fori_loop(0, nz, direct_build, 0)
            lax.fori_loop(1, ne, d_start, 0)
            own_d.start()
        grads(i * nz // far, (i + 1) * nz // far)
        if i == far - 1:
            gates_pass()
            direct_combine()
    store_in = pltpu.make_async_copy(gin, gin_hbm, st_sem.at[3])
    store_out = pltpu.make_async_copy(gout, gout_hbm, st_sem.at[4])
    store_in.start()
    store_out.start()

    def back_start(k, c):
        e = (me_e + k) % ne
        remote(back_send.at[e], back_recv.at[me_e], bk_ss.at[e], bk_rs.at[me_e], me_f, e).start()
        return c

    def back_wait(k, c):
        b = (me_e + ne - k) % ne
        remote(back_send.at[b], back_recv.at[b], bk_ss.at[b], bk_rs.at[b], me_f, b).wait_recv()
        return c

    for h in (0, 1):
        total = share(z, h)
        for d in (0, 1):
            last = hops(d, h) - 1
            rs_copy(d, h, last).wait_recv()
            total = total + rs_recv[d, h, last].astype(F32)
        back_send[h * he : (h + 1) * he] = total.astype(BF16)
    lax.fori_loop(1, ne, back_start, 0)
    own_back = pltpu.make_async_copy(back_send.at[me_e], back_recv.at[me_e], st_sem.at[5])
    own_back.start()

    def gf_wait(k, c):
        f = (me_f + nf - k) % nf
        remote(gf_all.at[f], gf_all.at[f], gf_ss.at[f], gf_rs.at[f], f, me_e).wait_recv()
        return c

    lax.fori_loop(1, nf, gf_wait, 0)
    total_gate = gf_all[0, :top, :]
    for f in range(1, nf):
        total_gate = total_gate + gf_all[f, :top, :]
    ogate_ref[...] = total_gate.astype(BF16)

    lax.fori_loop(1, nz, t_wait, 0)
    total = ts_send[z].astype(F32)
    for k in range(1, nz):
        total = total + ts_recv[(z + k) % nz].astype(F32)
    pair_send[:, :sub] = total

    lax.fori_loop(1, ne, back_wait, 0)
    own_back.wait()
    tok = tn(sel[...], flat(back_recv[...]))
    pair_send[:, sub:] = tok
    pair = remote(pair_send, pair_recv, pr_ss, pr_rs, pair_f, me_e)
    pair.start()
    pair.wait_recv()
    tok_all[z] = (pair_send[...] + pair_recv[...]).astype(BF16)

    hr = rows // 2

    def t_lead(buf, piece, h):
        return buf.at[piece, pl.ds(h * hr, hr)]

    ring(tok_all, t_lead, tr_ss, tr_rs, lambda i: None)
    for c in range(nz):
        out_ref[:, c * wz : (c + 1) * wz] = tok_all[c]

    def drain(k, c):
        e = (me_e + k) % ne
        x_copy(k).wait_send()
        remote(send_g.at[e], g_all.at[me_e], g_ss.at[e], g_rs.at[me_e], near_f(e), e).wait_send()
        remote(gs_send.at[e], gs_recv.at[me_e], gs_ss.at[e], gs_rs.at[me_e], me_f, e).wait_send()
        remote(d_send.at[e], d_recv.at[me_e], d_ss.at[e], d_rs.at[me_e], me_f, e).wait_send()
        remote(back_send.at[e], back_recv.at[me_e], bk_ss.at[e], bk_rs.at[me_e], me_f, e).wait_send()
        return c

    def drain_f(k, c):
        f = (me_f + k) % nf
        remote(gf_all.at[me_f], gf_all.at[me_f], gf_ss.at[f], gf_rs.at[me_f], f, me_e).wait_send()
        return c

    lax.fori_loop(1, ne, drain, 0)
    lax.fori_loop(1, nf, drain_f, 0)

    def drain_z(k, c):
        o = (z + k) % nz
        remote(
            ts_send.at[o], ts_recv.at[z], ts_ss.at[o], ts_rs.at[z], lo * nz + o, me_e
        ).wait_send()
        return c

    lax.fori_loop(1, nz, drain_z, 0)
    ring_drain(x_all, x_lead, xr_ss, xr_rs)

    def drain_swap(c, carry):
        for h in (0, 1):
            swap(c, h, lo).wait_send()
        return carry

    lax.fori_loop(0, nz, drain_swap, 0)
    ring_drain(tok_all, t_lead, tr_ss, tr_rs)
    for i in range(far):
        for h in (0, 1):
            for d in (0, 1):
                if i < hops(d, h):
                    rs_copy(d, h, i).wait_send()
    pair.wait_send()
    store_in.wait()
    store_out.wait()


def passing(a0, a1, a2, a3, o0, o1, o2, o3, b0, b1, b2, b3, sems):
    moves = []
    for n, (a, o, b) in enumerate(((a0, o0, b0), (a1, o1, b1), (a2, o2, b2), (a3, o3, b3))):
        pieces = PIECES if n > 1 else 1
        step = a.shape[0] // pieces
        for p in range(pieces):
            at = pl.ds(p * step, step)
            moves.append((
                pltpu.make_async_copy(a.at[at], b.at[at], sems.at[0, n, p]),
                pltpu.make_async_copy(b.at[at], o.at[at], sems.at[1, n, p]),
            ))
    for get, _ in moves:
        get.start()
    for get, put in moves:
        get.wait()
        put.start()
    for _, put in moves:
        put.wait()


def local(nf, ne, tokens, cotangent, expert_ids, gate_values, w_in, w_out):
    rows, width = tokens.shape
    top = expert_ids.shape[1]
    ff = w_in.shape[2]
    nz = nf // 2
    wz = width // nz
    far = nz // 2
    he = ne // 2
    dma = pltpu.SemaphoreType.DMA
    vmem = pl.BlockSpec(memory_space=pltpu.VMEM)
    hbm = pl.BlockSpec(memory_space=pl.ANY)
    ring_sems = dma((2, 2, far))
    out = pl.pallas_call(
        functools.partial(kernel, nf, ne),
        out_shape=(
            jax.ShapeDtypeStruct((rows, width), BF16),
            jax.ShapeDtypeStruct((top, rows), BF16),
            jax.ShapeDtypeStruct((width, ff), BF16),
            jax.ShapeDtypeStruct((ff, width), BF16),
        ),
        in_specs=[vmem, vmem, vmem, vmem, hbm, hbm],
        out_specs=(vmem, vmem, hbm, hbm),
        scratch_shapes=[
            pltpu.VMEM((width, ff), BF16),
            pltpu.VMEM((ff, width), BF16),
            pltpu.VMEM((ne, CAP, rows), F32),
            pltpu.VMEM((ne * CAP, rows), BF16),
            pltpu.VMEM((nz, ne * CAP, wz), BF16),
            pltpu.VMEM((ne * CAP, width), BF16),
            pltpu.VMEM((ne, CAP, wz + LANE), BF16),
            pltpu.VMEM((nz, ne, CAP, wz + LANE), BF16),
            pltpu.VMEM((ne, CAP, width - nz * LANE + LANE), BF16),
            pltpu.VMEM((ne, CAP, width - nz * LANE + LANE), BF16),
            pltpu.VMEM((ne * CAP, ff), F32),
            pltpu.VMEM((ne * CAP, ff), BF16),
            pltpu.VMEM((ne * CAP, ff), BF16),
            pltpu.VMEM((2, 2, he, CAP, wz - LANE), BF16),
            pltpu.VMEM((2, 2, far, he, CAP, wz - LANE), BF16),
            pltpu.VMEM((ne, CAP, wz - LANE), BF16),
            pltpu.VMEM((ne, CAP, wz - LANE), BF16),
            pltpu.VMEM((rows, wz), F32),
            pltpu.VMEM((rows, wz), F32),
            pltpu.VMEM((nz, rows, wz), BF16),
            pltpu.VMEM((ne, CAP, LANE), F32),
            pltpu.VMEM((ne, CAP, LANE), F32),
            pltpu.VMEM((nf, 8, rows), F32),
            pltpu.VMEM((width, ff), BF16),
            pltpu.VMEM((ff, width), BF16),
            pltpu.VMEM((ne, CAP, nz * LANE), BF16),
            pltpu.VMEM((ne, CAP, nz * LANE), BF16),
            pltpu.VMEM((nz, rows, LANE), BF16),
            pltpu.VMEM((nz, rows, LANE), BF16),
            dma((2,)),
            dma((ne,)), dma((ne,)), dma((ne,)), dma((ne,)),
            ring_sems, ring_sems, ring_sems, ring_sems,
            dma((ne,)), dma((ne,)),
            dma, dma,
            ring_sems, ring_sems,
            dma((ne,)), dma((ne,)),
            dma((nf,)), dma((nf,)),
            dma((ne,)), dma((ne,)), dma((nz,)), dma((nz,)),
            dma((nz, 2)), dma((nz, 2)),
            dma((7,)),
        ],
        compiler_params=pltpu.CompilerParams(
            collective_id=0, has_side_effects=True, vmem_limit_bytes=62 * 1024 * 1024
        ),
    )(
        tokens, cotangent, expert_ids.T, gate_values.T,
        w_in.reshape(width, ff), w_out.reshape(ff, width),
    )
    out = pl.pallas_call(
        passing,
        out_shape=tuple(jax.ShapeDtypeStruct(a.shape, a.dtype) for a in out),
        in_specs=[hbm] * 4,
        out_specs=(hbm,) * 4,
        scratch_shapes=[pltpu.VMEM(a.shape, a.dtype) for a in out] + [dma((2, 4, PIECES))],
        compiler_params=pltpu.CompilerParams(vmem_limit_bytes=62 * 1024 * 1024),
    )(*out)
    return (
        out[0],
        out[1].T,
        out[2].reshape(w_in.shape),
        out[3].reshape(w_out.shape),
    )


def solution(mesh):
    return jax.shard_map(
        functools.partial(local, mesh.shape["fsdp"], mesh.shape["expert"]),
        mesh=mesh,
        in_specs=(
            P("expert", None),
            P("expert", None),
            P("expert", None),
            P("expert", None),
            P(None, "expert", "fsdp"),
            P("fsdp", "expert", None),
        ),
        out_specs=(
            P("expert", None),
            P("expert", None),
            P(None, "expert", "fsdp"),
            P("fsdp", "expert", None),
        ),
        check_vma=False,
    )
```

```python
import functools

import jax
import jax.numpy as jnp
from jax import lax
from jax.experimental import pallas as pl
from jax.experimental.pallas import tpu as pltpu
from jax.sharding import PartitionSpec as P

CAP = 40
F32 = jnp.float32
BF16 = jnp.bfloat16
MESH = pl.DeviceIdType.MESH
LANE = 128
PIECES = 4


def nt(a, b):
    return lax.dot_general(a, b, (((1,), (1,)), ((), ())), preferred_element_type=F32)


def tn(a, b):
    return lax.dot_general(a, b, (((0,), (0,)), ((), ())), preferred_element_type=F32)


def flat(v):
    return v.astype(F32).reshape(v.shape[0] * v.shape[1], v.shape[2]).astype(BF16)


def blocks(v):
    return v.reshape(v.shape[0] // CAP, CAP, v.shape[1])


def kernel(
    nf, ne, tok_ref, cot_ref, ids_ref, gates_ref, win_hbm, wout_hbm,
    out_ref, ogate_ref, gin_hbm, gout_hbm,
    win, wout, sel32, sel, x2, g2, send_x, x_all, send_g, g_all, pre, gp16, ag16,
    rs_send, rs_recv, back_send, back_recv, pair_send, pair_recv, tok_all,
    gs_send, gs_recv, gf_all, gin, gout, d_send, d_recv, ts_send, ts_recv,
    load_sem, x_ss, x_rs, g_ss, g_rs, xr_ss, xr_rs, rs_ss, rs_rs, bk_ss, bk_rs,
    pr_ss, pr_rs, tr_ss, tr_rs, gs_ss, gs_rs, gf_ss, gf_rs, d_ss, d_rs, ts_ss, ts_rs, sw_ss, sw_rs, st_sem,
):
    me_f, me_e = lax.axis_index("fsdp"), lax.axis_index("expert")
    nz = nf // 2
    lo, z = me_f // nz, me_f % nz
    rows, width = tok_ref.shape
    wz = width // nz
    ff = win.shape[1]
    top = ids_ref.shape[0]
    slots = ne * CAP
    he, hs = ne // 2, slots // 2
    sub = LANE
    wr = wz - sub
    pair_f = (1 - lo) * nz + z
    right_f = lo * nz + (z + 1) % nz
    left_f = lo * nz + (z + nz - 1) % nz

    def dev(f, e):
        return {"fsdp": f, "expert": e}

    def remote(src, dst, ss, rs, f, e):
        return pltpu.make_async_remote_copy(
            src_ref=src, dst_ref=dst, send_sem=ss, recv_sem=rs,
            device_id=dev(f, e), device_id_type=MESH,
        )

    barrier = pltpu.get_barrier_semaphore()

    def greet_e(k, c):
        pl.semaphore_signal(barrier, inc=1, device_id=dev(me_f, (me_e + k) % ne), device_id_type=MESH)
        return c

    def greet_f(k, c):
        pl.semaphore_signal(barrier, inc=1, device_id=dev((me_f + k) % nf, me_e), device_id_type=MESH)
        return c

    lax.fori_loop(1, ne, greet_e, 0)
    lax.fori_loop(1, nf, greet_f, 0)
    load_in = pltpu.make_async_copy(win_hbm, win, load_sem.at[0])
    load_out = pltpu.make_async_copy(wout_hbm, wout, load_sem.at[1])
    load_in.start()
    load_out.start()

    ids = ids_ref[...]
    gates = gates_ref[...].astype(F32)
    exps = lax.broadcasted_iota(jnp.int32, (ne, rows), 0)
    named = jnp.zeros((ne, rows), F32)
    gate_of = jnp.zeros((ne, rows), F32)
    for k in range(top):
        hit = exps == ids[k : k + 1, :]
        named = named + jnp.where(hit, 1.0, 0.0)
        gate_of = gate_of + jnp.where(hit, gates[k : k + 1, :], 0.0)
    before = lax.broadcasted_iota(jnp.int32, (rows, rows), 0) < lax.broadcasted_iota(
        jnp.int32, (rows, rows), 1
    )
    place = jnp.dot(
        named.astype(BF16), jnp.where(before, 1.0, 0.0).astype(BF16), preferred_element_type=F32
    )
    place = jnp.where(named > 0.5, place, -1.0)
    slot_no = lax.broadcasted_iota(jnp.int32, (CAP, rows), 0).astype(F32)
    for e in range(ne):
        one = jnp.where(slot_no == place[e : e + 1, :], 1.0, 0.0)
        sel32[e] = one
        gate_col = jnp.sum(one * gate_of[e : e + 1, :], axis=1, keepdims=True)
        send_g[e, :, width:] = jnp.broadcast_to(gate_col, (CAP, LANE)).astype(BF16)
    sel[...] = sel32[...].reshape(slots, rows).astype(BF16)
    pick = sel[...]
    cols = pl.ds(pl.multiple_of(z * wz, LANE), wz)
    send_x[...] = blocks(jnp.dot(pick, tok_ref[:, cols], preferred_element_type=F32)).astype(BF16)

    pl.semaphore_wait(barrier, (ne - 1) + (nf - 1))

    def x_copy(k):
        e = (me_e + k) % ne
        return remote(send_x.at[e], x_all.at[z, me_e], x_ss.at[e], x_rs.at[me_e], me_f, e)

    def x_start(k, c):
        x_copy(k).start()
        return c

    lax.fori_loop(1, ne, x_start, 0)
    own_x = pltpu.make_async_copy(send_x.at[me_e], x_all.at[z, me_e], st_sem.at[0])
    own_x.start()

    gw = width // 6 if width % (6 * LANE) == 0 else width

    def g_build(j, c):
        span = pl.ds(pl.multiple_of(j * gw, LANE), gw)
        send_g[:, :, span] = blocks(
            jnp.dot(sel[...], cot_ref[:, span], preferred_element_type=F32)
        ).astype(BF16)
        return c

    lax.fori_loop(0, width // gw, g_build, 0)

    def g_start(k, c):
        e = (me_e + k) % ne
        remote(send_g.at[e], g_all.at[me_e], g_ss.at[e], g_rs.at[me_e], me_f, e).start()
        return c

    own_g = pltpu.make_async_copy(send_g.at[me_e], g_all.at[me_e], st_sem.at[1])
    own_g.start()

    def x_wait(k, c):
        b = (me_e + ne - k) % ne
        remote(send_x.at[b], x_all.at[z, b], x_ss.at[b], x_rs.at[b], me_f, b).wait_recv()
        return c

    lax.fori_loop(1, ne, x_wait, 0)
    own_x.wait()
    lax.fori_loop(1, ne, g_start, 0)

    far = nz // 2

    def hops(direction, h):
        return far if direction == h else far - 1

    def ring_copy(buf, lead, ss, rs, direction, h, i):
        piece = (z + nz - i) % nz if direction == 0 else (z + i) % nz
        ref = lead(buf, piece, h)
        return remote(
            ref, ref, ss.at[direction, h, i], rs.at[direction, h, i],
            right_f if direction == 0 else left_f, me_e,
        )

    def ring_arrival(buf, lead, ss, rs, direction, h, i):
        piece = (z + nz - 1 - i) % nz if direction == 0 else (z + 1 + i) % nz
        ref = lead(buf, piece, h)
        return remote(
            ref, ref, ss.at[direction, h, i], rs.at[direction, h, i],
            right_f if direction == 0 else left_f, me_e,
        )

    def ring(buf, lead, ss, rs, between, arrived=None):
        for i in range(far + 1):
            for h in (0, 1):
                for d in (0, 1):
                    if 0 < i <= hops(d, h):
                        ring_arrival(buf, lead, ss, rs, d, h, i - 1).wait_recv()
                    if i < hops(d, h):
                        ring_copy(buf, lead, ss, rs, d, h, i).start()
                    if arrived is not None and 0 < i <= hops(d, h):
                        arrived((z + nz - i) % nz if d == 0 else (z + i) % nz, h)
            between(i)

    def ring_drain(buf, lead, ss, rs):
        for i in range(far):
            for h in (0, 1):
                for d in (0, 1):
                    if i < hops(d, h):
                        ring_copy(buf, lead, ss, rs, d, h, i).wait_send()

    def x_lead(buf, piece, h):
        return buf.at[piece, pl.ds(h * he, he)]

    def add_pre(c):
        w_rows = win[pl.ds(pl.multiple_of(c * wz, LANE), wz), :]
        for h in (0, 1):
            xs = flat(x_all[c, h * he : (h + 1) * he])
            x2[c, h * hs : (h + 1) * hs, :] = xs
            pre[h * hs : (h + 1) * hs, :] += jnp.dot(xs, w_rows, preferred_element_type=F32)

    pre[...] = jnp.zeros_like(pre)

    def x_between(i):
        if i == 0:
            load_in.wait()
            add_pre(z)
            return
        add_pre((z + nz - i) % nz)
        if i < far:
            add_pre((z + i) % nz)

    ring(x_all, x_lead, xr_ss, xr_rs, x_between)

    def g_arrival(b):
        return remote(send_g.at[b], g_all.at[b], g_ss.at[b], g_rs.at[b], me_f, b)

    def g_flat(p):
        g2[pl.ds(pl.multiple_of(p * 2 * CAP, 16), 2 * CAP), :] = flat(
            g_all[pl.ds(2 * p, 2), :, :width]
        )

    own_g.wait()
    g_arrival(me_e + 1 - 2 * (me_e % 2)).wait_recv()
    g_flat(me_e // 2)

    def g_take(k, c):
        p = (me_e // 2 + he - k) % he
        g_arrival(2 * p).wait_recv()
        g_arrival(2 * p + 1).wait_recv()
        g_flat(p)
        return c

    lax.fori_loop(1, he, g_take, 0)
    load_out.wait()

    for h in (0, 1):
        span = slice(h * hs, (h + 1) * hs)
        up = nt(g2[span, :], wout[...])
        gate = g_all[h * he : (h + 1) * he, :, width:].astype(F32).reshape(hs, LANE)
        gate = jnp.concatenate([gate] * (ff // LANE), axis=1)
        p = pre[span, :]
        squash = jax.nn.sigmoid(p)
        active = p * squash
        part = jnp.sum(active * up, axis=1, keepdims=True)
        gs_send[h * he : (h + 1) * he] = blocks(jnp.broadcast_to(part, (hs, LANE)))
        ag16[span, :] = (gate * active).astype(BF16)
        gp16[span, :] = (gate * squash * (1.0 + p * (1.0 - squash)) * up).astype(BF16)

    def share(c, h):
        part = win[pl.ds(pl.multiple_of(c * wz + sub, LANE), wr), :]
        return blocks(nt(gp16[h * hs : (h + 1) * hs, :], part))

    def direct_build(c, carry):
        part = win[pl.ds(pl.multiple_of(c * wz, LANE), sub), :]
        d_send[:, :, pl.ds(pl.multiple_of(c * sub, LANE), sub)] = blocks(
            nt(gp16[...], part)
        ).astype(BF16)
        return carry

    def d_start(k, c):
        e = (me_e + k) % ne
        remote(d_send.at[e], d_recv.at[me_e], d_ss.at[e], d_rs.at[me_e], me_f, e).start()
        return c

    def d_wait(k, c):
        b = (me_e + ne - k) % ne
        remote(d_send.at[b], d_recv.at[b], d_ss.at[b], d_rs.at[b], me_f, b).wait_recv()
        return c

    def t_start(k, c):
        o = (z + k) % nz
        remote(
            ts_send.at[o], ts_recv.at[z], ts_ss.at[o], ts_rs.at[z], lo * nz + o, me_e
        ).start()
        return c

    def t_wait(k, c):
        o = (z + nz - k) % nz
        remote(
            ts_send.at[o], ts_recv.at[o], ts_ss.at[o], ts_rs.at[o], lo * nz + o, me_e
        ).wait_recv()
        return c

    def direct_combine():
        lax.fori_loop(1, ne, d_wait, 0)
        own_d.wait()

        def one(c, carry):
            part = flat(d_recv[:, :, pl.ds(pl.multiple_of(c * sub, LANE), sub)])
            ts_send[c] = tn(sel[...], part).astype(BF16)
            return carry

        lax.fori_loop(0, nz, one, 0)
        lax.fori_loop(1, nz, t_start, 0)

    own_d = pltpu.make_async_copy(d_send.at[me_e], d_recv.at[me_e], st_sem.at[6])

    def rs_src(d, h, i):
        return rs_send.at[d, h] if i == 0 else rs_recv.at[d, h, i - 1]

    def rs_copy(d, h, i):
        return remote(
            rs_src(d, h, i), rs_recv.at[d, h, i], rs_ss.at[d, h, i], rs_rs.at[d, h, i],
            right_f if d == 0 else left_f, me_e,
        )

    def rs_step(d, h, i):
        n = hops(d, h)
        c = (z + n - i) % nz if d == 0 else (z + nz - (n - i)) % nz
        total = share(c, h)
        if i > 0:
            rs_copy(d, h, i - 1).wait_recv()
            total = total + rs_src(d, h, i)[...].astype(F32)
        rs_src(d, h, i)[...] = total.astype(BF16)
        rs_copy(d, h, i).start()

    def gs_start(k, c):
        e = (me_e + k) % ne
        remote(gs_send.at[e], gs_recv.at[me_e], gs_ss.at[e], gs_rs.at[me_e], me_f, e).start()
        return c

    def gs_wait(k, c):
        b = (me_e + ne - k) % ne
        remote(gs_send.at[b], gs_recv.at[b], gs_ss.at[b], gs_rs.at[b], me_f, b).wait_recv()
        return c

    def grad_in_piece(c):
        gin[pl.ds(pl.multiple_of(c * wz, LANE), wz), :] = tn(
            x2[c], gp16[...]
        ).astype(BF16)

    def grad_out_piece(c):
        span = pl.ds(pl.multiple_of(c * wz, LANE), wz)
        gout[:, span] = tn(
            ag16[...], g2[:, span]
        ).astype(BF16)

    def grads(first, last):
        def one(c, carry):
            grad_in_piece(c)
            grad_out_piece(c)
            return carry

        lax.fori_loop(first, last, one, 0)

    def gates_pass():
        lax.fori_loop(1, ne, gs_wait, 0)
        own_gs.wait()
        acc = jnp.zeros((top, rows), F32)
        for e in range(ne):
            row = jnp.sum(sel32[e] * gs_recv[e], axis=0, keepdims=True)
            acc = acc + jnp.where(ids_ref[...] == e, row, 0.0)
        gf_all[me_f, :top, :] = acc

        def gf_start(k, c):
            f = (me_f + k) % nf
            remote(gf_all.at[me_f], gf_all.at[me_f], gf_ss.at[f], gf_rs.at[me_f], f, me_e).start()
            return c

        lax.fori_loop(1, nf, gf_start, 0)

    own_gs = pltpu.make_async_copy(gs_send.at[me_e], gs_recv.at[me_e], st_sem.at[2])
    for i in range(far):
        for h in (0, 1):
            for d in (0, 1):
                if i < hops(d, h):
                    rs_step(d, h, i)
        if i == 0:
            lax.fori_loop(1, ne, gs_start, 0)
            own_gs.start()
            lax.fori_loop(0, nz, direct_build, 0)
            lax.fori_loop(1, ne, d_start, 0)
            own_d.start()
        grads(i * nz // far, (i + 1) * nz // far)
        if i == far - 1:
            gates_pass()
            direct_combine()
    store_in = pltpu.make_async_copy(gin, gin_hbm, st_sem.at[3])
    store_out = pltpu.make_async_copy(gout, gout_hbm, st_sem.at[4])
    store_in.start()
    store_out.start()

    def back_start(k, c):
        e = (me_e + k) % ne
        remote(back_send.at[e], back_recv.at[me_e], bk_ss.at[e], bk_rs.at[me_e], me_f, e).start()
        return c

    def back_wait(k, c):
        b = (me_e + ne - k) % ne
        remote(back_send.at[b], back_recv.at[b], bk_ss.at[b], bk_rs.at[b], me_f, b).wait_recv()
        return c

    for h in (0, 1):
        total = share(z, h)
        for d in (0, 1):
            last = hops(d, h) - 1
            rs_copy(d, h, last).wait_recv()
            total = total + rs_recv[d, h, last].astype(F32)
        back_send[h * he : (h + 1) * he] = total.astype(BF16)
    lax.fori_loop(1, ne, back_start, 0)
    own_back = pltpu.make_async_copy(back_send.at[me_e], back_recv.at[me_e], st_sem.at[5])
    own_back.start()

    def gf_wait(k, c):
        f = (me_f + nf - k) % nf
        remote(gf_all.at[f], gf_all.at[f], gf_ss.at[f], gf_rs.at[f], f, me_e).wait_recv()
        return c

    lax.fori_loop(1, nf, gf_wait, 0)
    total_gate = gf_all[0, :top, :]
    for f in range(1, nf):
        total_gate = total_gate + gf_all[f, :top, :]
    ogate_ref[...] = total_gate.astype(BF16)

    lax.fori_loop(1, nz, t_wait, 0)
    total = ts_send[z].astype(F32)
    for k in range(1, nz):
        total = total + ts_recv[(z + k) % nz].astype(F32)
    pair_send[:, :sub] = total

    lax.fori_loop(1, ne, back_wait, 0)
    own_back.wait()
    tok = tn(sel[...], flat(back_recv[...]))
    pair_send[:, sub:] = tok
    hr = rows // 2
    mine = pl.ds(pl.multiple_of(lo * hr, 16), hr)
    other = pl.ds(pl.multiple_of((1 - lo) * hr, 16), hr)
    pair = remote(pair_send.at[other], pair_recv.at[other], pr_ss, pr_rs, pair_f, me_e)
    pair.start()
    remote(pair_send.at[mine], pair_recv.at[mine], pr_ss, pr_rs, pair_f, me_e).wait_recv()
    tok_all[z, mine, :] = (pair_send[mine, :] + pair_recv[mine, :]).astype(BF16)

    def t_rows(piece, l, h):
        return tok_all.at[piece, pl.ds(pl.multiple_of(l * hr + h * (hr // 2), 16), hr // 2)]

    def t_lead(buf, piece, h):
        return t_rows(piece, lo, h)

    def swap(c, h, l):
        ref = t_rows(c, l, h)
        return remote(ref, ref, sw_ss.at[c, h], sw_rs.at[c, h], pair_f, me_e)

    def t_between(i):
        if i == 0:
            swap(z, 0, lo).start()
            swap(z, 1, lo).start()

    ring(tok_all, t_lead, tr_ss, tr_rs, t_between, lambda c, h: swap(c, h, lo).start())
    for i in range(nz):
        c = (z + (0, 1, nz - 1, 2, nz - 2, 3, nz - 3, 4)[i]) % nz if nz == 8 else i
        for h in (0, 1):
            swap(c, h, 1 - lo).wait_recv()
    for c in range(nz):
        out_ref[:, c * wz : (c + 1) * wz] = tok_all[c]

    def drain(k, c):
        e = (me_e + k) % ne
        remote(send_x.at[e], x_all.at[z, me_e], x_ss.at[e], x_rs.at[me_e], me_f, e).wait_send()
        remote(send_g.at[e], g_all.at[me_e], g_ss.at[e], g_rs.at[me_e], me_f, e).wait_send()
        remote(gs_send.at[e], gs_recv.at[me_e], gs_ss.at[e], gs_rs.at[me_e], me_f, e).wait_send()
        remote(d_send.at[e], d_recv.at[me_e], d_ss.at[e], d_rs.at[me_e], me_f, e).wait_send()
        remote(back_send.at[e], back_recv.at[me_e], bk_ss.at[e], bk_rs.at[me_e], me_f, e).wait_send()
        return c

    def drain_f(k, c):
        f = (me_f + k) % nf
        remote(gf_all.at[me_f], gf_all.at[me_f], gf_ss.at[f], gf_rs.at[me_f], f, me_e).wait_send()
        return c

    lax.fori_loop(1, ne, drain, 0)
    lax.fori_loop(1, nf, drain_f, 0)

    def drain_z(k, c):
        o = (z + k) % nz
        remote(
            ts_send.at[o], ts_recv.at[z], ts_ss.at[o], ts_rs.at[z], lo * nz + o, me_e
        ).wait_send()
        return c

    lax.fori_loop(1, nz, drain_z, 0)
    ring_drain(x_all, x_lead, xr_ss, xr_rs)
    ring_drain(tok_all, t_lead, tr_ss, tr_rs)

    def drain_swap(c, carry):
        for h in (0, 1):
            swap(c, h, lo).wait_send()
        return carry

    lax.fori_loop(0, nz, drain_swap, 0)
    for i in range(far):
        for h in (0, 1):
            for d in (0, 1):
                if i < hops(d, h):
                    rs_copy(d, h, i).wait_send()
    pair.wait_send()
    store_in.wait()
    store_out.wait()


def passing(a0, a1, a2, a3, o0, o1, o2, o3, b0, b1, b2, b3, sems):
    moves = []
    for n, (a, o, b) in enumerate(((a0, o0, b0), (a1, o1, b1), (a2, o2, b2), (a3, o3, b3))):
        pieces = PIECES if n > 1 else 1
        step = a.shape[0] // pieces
        for p in range(pieces):
            at = pl.ds(p * step, step)
            moves.append((
                pltpu.make_async_copy(a.at[at], b.at[at], sems.at[0, n, p]),
                pltpu.make_async_copy(b.at[at], o.at[at], sems.at[1, n, p]),
            ))
    for get, _ in moves:
        get.start()
    for get, put in moves:
        get.wait()
        put.start()
    for _, put in moves:
        put.wait()


def local(nf, ne, tokens, cotangent, expert_ids, gate_values, w_in, w_out):
    rows, width = tokens.shape
    top = expert_ids.shape[1]
    ff = w_in.shape[2]
    nz = nf // 2
    wz = width // nz
    far = nz // 2
    he = ne // 2
    dma = pltpu.SemaphoreType.DMA
    vmem = pl.BlockSpec(memory_space=pltpu.VMEM)
    hbm = pl.BlockSpec(memory_space=pl.ANY)
    ring_sems = dma((2, 2, far))
    out = pl.pallas_call(
        functools.partial(kernel, nf, ne),
        out_shape=(
            jax.ShapeDtypeStruct((rows, width), BF16),
            jax.ShapeDtypeStruct((top, rows), BF16),
            jax.ShapeDtypeStruct((width, ff), BF16),
            jax.ShapeDtypeStruct((ff, width), BF16),
        ),
        in_specs=[vmem, vmem, vmem, vmem, hbm, hbm],
        out_specs=(vmem, vmem, hbm, hbm),
        scratch_shapes=[
            pltpu.VMEM((width, ff), BF16),
            pltpu.VMEM((ff, width), BF16),
            pltpu.VMEM((ne, CAP, rows), F32),
            pltpu.VMEM((ne * CAP, rows), BF16),
            pltpu.VMEM((nz, ne * CAP, wz), BF16),
            pltpu.VMEM((ne * CAP, width), BF16),
            pltpu.VMEM((ne, CAP, wz), BF16),
            pltpu.VMEM((nz, ne, CAP, wz), BF16),
            pltpu.VMEM((ne, CAP, width + LANE), BF16),
            pltpu.VMEM((ne, CAP, width + LANE), BF16),
            pltpu.VMEM((ne * CAP, ff), F32),
            pltpu.VMEM((ne * CAP, ff), BF16),
            pltpu.VMEM((ne * CAP, ff), BF16),
            pltpu.VMEM((2, 2, he, CAP, wz - LANE), BF16),
            pltpu.VMEM((2, 2, far, he, CAP, wz - LANE), BF16),
            pltpu.VMEM((ne, CAP, wz - LANE), BF16),
            pltpu.VMEM((ne, CAP, wz - LANE), BF16),
            pltpu.VMEM((rows, wz), F32),
            pltpu.VMEM((rows, wz), F32),
            pltpu.VMEM((nz, rows, wz), BF16),
            pltpu.VMEM((ne, CAP, LANE), F32),
            pltpu.VMEM((ne, CAP, LANE), F32),
            pltpu.VMEM((nf, 8, rows), F32),
            pltpu.VMEM((width, ff), BF16),
            pltpu.VMEM((ff, width), BF16),
            pltpu.VMEM((ne, CAP, nz * LANE), BF16),
            pltpu.VMEM((ne, CAP, nz * LANE), BF16),
            pltpu.VMEM((nz, rows, LANE), BF16),
            pltpu.VMEM((nz, rows, LANE), BF16),
            dma((2,)),
            dma((ne,)), dma((ne,)), dma((ne,)), dma((ne,)),
            ring_sems, ring_sems, ring_sems, ring_sems,
            dma((ne,)), dma((ne,)),
            dma, dma,
            ring_sems, ring_sems,
            dma((ne,)), dma((ne,)),
            dma((nf,)), dma((nf,)),
            dma((ne,)), dma((ne,)), dma((nz,)), dma((nz,)),
            dma((nz, 2)), dma((nz, 2)),
            dma((7,)),
        ],
        compiler_params=pltpu.CompilerParams(
            collective_id=0, has_side_effects=True, vmem_limit_bytes=62 * 1024 * 1024
        ),
    )(
        tokens, cotangent, expert_ids.T, gate_values.T,
        w_in.reshape(width, ff), w_out.reshape(ff, width),
    )
    out = pl.pallas_call(
        passing,
        out_shape=tuple(jax.ShapeDtypeStruct(a.shape, a.dtype) for a in out),
        in_specs=[hbm] * 4,
        out_specs=(hbm,) * 4,
        scratch_shapes=[pltpu.VMEM(a.shape, a.dtype) for a in out] + [dma((2, 4, PIECES))],
        compiler_params=pltpu.CompilerParams(vmem_limit_bytes=62 * 1024 * 1024),
    )(*out)
    return (
        out[0],
        out[1].T,
        out[2].reshape(w_in.shape),
        out[3].reshape(w_out.shape),
    )


def solution(mesh):
    return jax.shard_map(
        functools.partial(local, mesh.shape["fsdp"], mesh.shape["expert"]),
        mesh=mesh,
        in_specs=(
            P("expert", None),
            P("expert", None),
            P("expert", None),
            P("expert", None),
            P(None, "expert", "fsdp"),
            P("fsdp", "expert", None),
        ),
        out_specs=(
            P("expert", None),
            P("expert", None),
            P(None, "expert", "fsdp"),
            P("fsdp", "expert", None),
        ),
        check_vma=False,
    )
```

```python
import functools

import jax
import jax.numpy as jnp
from jax import lax
from jax.experimental import pallas as pl
from jax.experimental.pallas import tpu as pltpu
from jax.sharding import PartitionSpec as P

CAP = 40
F32 = jnp.float32
BF16 = jnp.bfloat16
MESH = pl.DeviceIdType.MESH
LANE = 128
PIECES = 4


def nt(a, b):
    return lax.dot_general(a, b, (((1,), (1,)), ((), ())), preferred_element_type=F32)


def tn(a, b):
    return lax.dot_general(a, b, (((0,), (0,)), ((), ())), preferred_element_type=F32)


def flat(v):
    return v.astype(F32).reshape(v.shape[0] * v.shape[1], v.shape[2]).astype(BF16)


def blocks(v):
    return v.reshape(v.shape[0] // CAP, CAP, v.shape[1])


def kernel(
    nf, ne, tok_ref, cot_ref, ids_ref, gates_ref, win_hbm, wout_hbm,
    out_ref, ogate_ref, gin_hbm, gout_hbm,
    win, wout, sel32, sel, x2, g2, send_x, x_all, send_g, g_all, pre, gp16, ag16,
    rs_send, rs_recv, back_send, back_recv, pair_send, pair_recv, tok_all,
    gs_send, gs_recv, gf_all, gin, gout, d_send, d_recv, ts_send, ts_recv,
    load_sem, x_ss, x_rs, g_ss, g_rs, xr_ss, xr_rs, rs_ss, rs_rs, bk_ss, bk_rs,
    pr_ss, pr_rs, tr_ss, tr_rs, gs_ss, gs_rs, gf_ss, gf_rs, d_ss, d_rs, ts_ss, ts_rs, sw_ss, sw_rs, st_sem,
):
    me_f, me_e = lax.axis_index("fsdp"), lax.axis_index("expert")
    nz = nf // 2
    lo, z = me_f // nz, me_f % nz
    rows, width = tok_ref.shape
    wz = width // nz
    ff = win.shape[1]
    top = ids_ref.shape[0]
    slots = ne * CAP
    he, hs = ne // 2, slots // 2
    sub = LANE
    wr = wz - sub
    pair_f = (1 - lo) * nz + z
    right_f = lo * nz + (z + 1) % nz
    left_f = lo * nz + (z + nz - 1) % nz

    def dev(f, e):
        return {"fsdp": f, "expert": e}

    def remote(src, dst, ss, rs, f, e):
        return pltpu.make_async_remote_copy(
            src_ref=src, dst_ref=dst, send_sem=ss, recv_sem=rs,
            device_id=dev(f, e), device_id_type=MESH,
        )

    barrier = pltpu.get_barrier_semaphore()

    def greet_e(k, c):
        pl.semaphore_signal(barrier, inc=1, device_id=dev(me_f, (me_e + k) % ne), device_id_type=MESH)
        return c

    def greet_f(k, c):
        pl.semaphore_signal(barrier, inc=1, device_id=dev((me_f + k) % nf, me_e), device_id_type=MESH)
        return c

    lax.fori_loop(1, ne, greet_e, 0)
    lax.fori_loop(1, nf, greet_f, 0)
    load_in = pltpu.make_async_copy(win_hbm, win, load_sem.at[0])
    load_out = pltpu.make_async_copy(wout_hbm, wout, load_sem.at[1])
    load_in.start()
    load_out.start()

    ids = ids_ref[...]
    gates = gates_ref[...].astype(F32)
    exps = lax.broadcasted_iota(jnp.int32, (ne, rows), 0)
    named = jnp.zeros((ne, rows), F32)
    gate_of = jnp.zeros((ne, rows), F32)
    for k in range(top):
        hit = exps == ids[k : k + 1, :]
        named = named + jnp.where(hit, 1.0, 0.0)
        gate_of = gate_of + jnp.where(hit, gates[k : k + 1, :], 0.0)
    before = lax.broadcasted_iota(jnp.int32, (rows, rows), 0) < lax.broadcasted_iota(
        jnp.int32, (rows, rows), 1
    )
    place = jnp.dot(
        named.astype(BF16), jnp.where(before, 1.0, 0.0).astype(BF16), preferred_element_type=F32
    )
    place = jnp.where(named > 0.5, place, -1.0)
    slot_no = lax.broadcasted_iota(jnp.int32, (CAP, rows), 0).astype(F32)
    for e in range(ne):
        one = jnp.where(slot_no == place[e : e + 1, :], 1.0, 0.0)
        sel32[e] = one
        gate_col = jnp.sum(one * gate_of[e : e + 1, :], axis=1, keepdims=True)
        send_g[e, :, width:] = jnp.broadcast_to(gate_col, (CAP, LANE)).astype(BF16)
    sel[...] = sel32[...].reshape(slots, rows).astype(BF16)
    pick = sel[...]
    cols = pl.ds(pl.multiple_of(z * wz, LANE), wz)
    send_x[...] = blocks(jnp.dot(pick, tok_ref[:, cols], preferred_element_type=F32)).astype(BF16)

    pl.semaphore_wait(barrier, (ne - 1) + (nf - 1))

    def x_copy(k):
        e = (me_e + k) % ne
        return remote(send_x.at[e], x_all.at[z, me_e], x_ss.at[e], x_rs.at[me_e], me_f, e)

    def x_start(k, c):
        x_copy(k).start()
        return c

    lax.fori_loop(1, ne, x_start, 0)
    own_x = pltpu.make_async_copy(send_x.at[me_e], x_all.at[z, me_e], st_sem.at[0])
    own_x.start()

    gw = width // 6 if width % (6 * LANE) == 0 else width

    def g_build(j, c):
        span = pl.ds(pl.multiple_of(j * gw, LANE), gw)
        send_g[:, :, span] = blocks(
            jnp.dot(sel[...], cot_ref[:, span], preferred_element_type=F32)
        ).astype(BF16)
        return c

    lax.fori_loop(0, width // gw, g_build, 0)

    def g_start(k, c):
        e = (me_e + k) % ne
        remote(send_g.at[e], g_all.at[me_e], g_ss.at[e], g_rs.at[me_e], me_f, e).start()
        return c

    own_g = pltpu.make_async_copy(send_g.at[me_e], g_all.at[me_e], st_sem.at[1])
    own_g.start()

    def x_wait(k, c):
        b = (me_e + ne - k) % ne
        remote(send_x.at[b], x_all.at[z, b], x_ss.at[b], x_rs.at[b], me_f, b).wait_recv()
        return c

    lax.fori_loop(1, ne, x_wait, 0)
    own_x.wait()
    lax.fori_loop(1, ne, g_start, 0)

    far = nz // 2

    def hops(direction, h):
        return far if direction == h else far - 1

    def ring_copy(buf, lead, ss, rs, direction, h, i):
        piece = (z + nz - i) % nz if direction == 0 else (z + i) % nz
        ref = lead(buf, piece, h)
        return remote(
            ref, ref, ss.at[direction, h, i], rs.at[direction, h, i],
            right_f if direction == 0 else left_f, me_e,
        )

    def ring_arrival(buf, lead, ss, rs, direction, h, i):
        piece = (z + nz - 1 - i) % nz if direction == 0 else (z + 1 + i) % nz
        ref = lead(buf, piece, h)
        return remote(
            ref, ref, ss.at[direction, h, i], rs.at[direction, h, i],
            right_f if direction == 0 else left_f, me_e,
        )

    def ring(buf, lead, ss, rs, between, arrived=None):
        for i in range(far + 1):
            for h in (0, 1):
                for d in (0, 1):
                    if 0 < i <= hops(d, h):
                        ring_arrival(buf, lead, ss, rs, d, h, i - 1).wait_recv()
                    if i < hops(d, h):
                        ring_copy(buf, lead, ss, rs, d, h, i).start()
                    if arrived is not None and 0 < i <= hops(d, h):
                        arrived((z + nz - i) % nz if d == 0 else (z + i) % nz, h)
            between(i)

    def ring_drain(buf, lead, ss, rs):
        for i in range(far):
            for h in (0, 1):
                for d in (0, 1):
                    if i < hops(d, h):
                        ring_copy(buf, lead, ss, rs, d, h, i).wait_send()

    def x_lead(buf, piece, h):
        return buf.at[piece, pl.ds(h * he, he)]

    def add_pre(c):
        w_rows = win[pl.ds(pl.multiple_of(c * wz, LANE), wz), :]
        for h in (0, 1):
            xs = flat(x_all[c, h * he : (h + 1) * he])
            x2[c, h * hs : (h + 1) * hs, :] = xs
            pre[h * hs : (h + 1) * hs, :] += jnp.dot(xs, w_rows, preferred_element_type=F32)

    pre[...] = jnp.zeros_like(pre)

    def x_between(i):
        if i == 0:
            load_in.wait()
            add_pre(z)
            return
        add_pre((z + nz - i) % nz)
        if i < far:
            add_pre((z + i) % nz)

    ring(x_all, x_lead, xr_ss, xr_rs, x_between)

    def g_arrival(b):
        return remote(send_g.at[b], g_all.at[b], g_ss.at[b], g_rs.at[b], me_f, b)

    def g_flat(p):
        g2[pl.ds(pl.multiple_of(p * 2 * CAP, 16), 2 * CAP), :] = flat(
            g_all[pl.ds(2 * p, 2), :, :width]
        )

    own_g.wait()
    g_arrival(me_e + 1 - 2 * (me_e % 2)).wait_recv()
    g_flat(me_e // 2)

    def g_take(k, c):
        p = (me_e // 2 + he - k) % he
        g_arrival(2 * p).wait_recv()
        g_arrival(2 * p + 1).wait_recv()
        g_flat(p)
        return c

    lax.fori_loop(1, he, g_take, 0)
    load_out.wait()

    for h in (0, 1):
        span = slice(h * hs, (h + 1) * hs)
        up = nt(g2[span, :], wout[...])
        gate = g_all[h * he : (h + 1) * he, :, width:].astype(F32).reshape(hs, LANE)
        gate = jnp.concatenate([gate] * (ff // LANE), axis=1)
        p = pre[span, :]
        squash = jax.nn.sigmoid(p)
        active = p * squash
        part = jnp.sum(active * up, axis=1, keepdims=True)
        gs_send[h * he : (h + 1) * he] = blocks(jnp.broadcast_to(part, (hs, LANE)))
        ag16[span, :] = (gate * active).astype(BF16)
        gp16[span, :] = (gate * squash * (1.0 + p * (1.0 - squash)) * up).astype(BF16)

    def share(c, h):
        part = win[pl.ds(pl.multiple_of(c * wz + sub, LANE), wr), :]
        return blocks(nt(gp16[h * hs : (h + 1) * hs, :], part))

    def direct_build(c, carry):
        part = win[pl.ds(pl.multiple_of(c * wz, LANE), sub), :]
        d_send[:, :, pl.ds(pl.multiple_of(c * sub, LANE), sub)] = blocks(
            nt(gp16[...], part)
        ).astype(BF16)
        return carry

    def d_start(k, c):
        e = (me_e + k) % ne
        remote(d_send.at[e], d_recv.at[me_e], d_ss.at[e], d_rs.at[me_e], me_f, e).start()
        return c

    def d_wait(k, c):
        b = (me_e + ne - k) % ne
        remote(d_send.at[b], d_recv.at[b], d_ss.at[b], d_rs.at[b], me_f, b).wait_recv()
        return c

    def t_start(k, c):
        o = (z + k) % nz
        remote(
            ts_send.at[o], ts_recv.at[z], ts_ss.at[o], ts_rs.at[z], lo * nz + o, me_e
        ).start()
        return c

    def t_wait(k, c):
        o = (z + nz - k) % nz
        remote(
            ts_send.at[o], ts_recv.at[o], ts_ss.at[o], ts_rs.at[o], lo * nz + o, me_e
        ).wait_recv()
        return c

    def direct_combine():
        lax.fori_loop(1, ne, d_wait, 0)
        own_d.wait()

        def one(c, carry):
            part = flat(d_recv[:, :, pl.ds(pl.multiple_of(c * sub, LANE), sub)])
            ts_send[c] = tn(sel[...], part).astype(BF16)
            return carry

        lax.fori_loop(0, nz, one, 0)
        lax.fori_loop(1, nz, t_start, 0)

    own_d = pltpu.make_async_copy(d_send.at[me_e], d_recv.at[me_e], st_sem.at[6])

    def rs_src(d, h, i):
        return rs_send.at[d, h] if i == 0 else rs_recv.at[d, h, i - 1]

    def rs_copy(d, h, i):
        return remote(
            rs_src(d, h, i), rs_recv.at[d, h, i], rs_ss.at[d, h, i], rs_rs.at[d, h, i],
            right_f if d == 0 else left_f, me_e,
        )

    def rs_step(d, h, i):
        n = hops(d, h)
        c = (z + n - i) % nz if d == 0 else (z + nz - (n - i)) % nz
        total = share(c, h)
        if i > 0:
            rs_copy(d, h, i - 1).wait_recv()
            total = total + rs_src(d, h, i)[...].astype(F32)
        rs_src(d, h, i)[...] = total.astype(BF16)
        rs_copy(d, h, i).start()

    def gs_start(k, c):
        e = (me_e + k) % ne
        remote(gs_send.at[e], gs_recv.at[me_e], gs_ss.at[e], gs_rs.at[me_e], me_f, e).start()
        return c

    def gs_wait(k, c):
        b = (me_e + ne - k) % ne
        remote(gs_send.at[b], gs_recv.at[b], gs_ss.at[b], gs_rs.at[b], me_f, b).wait_recv()
        return c

    def grad_in_piece(c):
        gin[pl.ds(pl.multiple_of(c * wz, LANE), wz), :] = tn(
            x2[c], gp16[...]
        ).astype(BF16)

    def grad_out_piece(c):
        span = pl.ds(pl.multiple_of(c * wz, LANE), wz)
        gout[:, span] = tn(
            ag16[...], g2[:, span]
        ).astype(BF16)

    def grads(first, last):
        def one(c, carry):
            grad_in_piece(c)
            grad_out_piece(c)
            return carry

        lax.fori_loop(first, last, one, 0)

    def gates_pass():
        lax.fori_loop(1, ne, gs_wait, 0)
        own_gs.wait()
        acc = jnp.zeros((top, rows), F32)
        for e in range(ne):
            row = jnp.sum(sel32[e] * gs_recv[e], axis=0, keepdims=True)
            acc = acc + jnp.where(ids_ref[...] == e, row, 0.0)
        gf_all[me_f, :top, :] = acc

        def gf_start(k, c):
            f = (me_f + k) % nf
            remote(gf_all.at[me_f], gf_all.at[me_f], gf_ss.at[f], gf_rs.at[me_f], f, me_e).start()
            return c

        lax.fori_loop(1, nf, gf_start, 0)

    own_gs = pltpu.make_async_copy(gs_send.at[me_e], gs_recv.at[me_e], st_sem.at[2])
    for i in range(far):
        for h in (0, 1):
            for d in (0, 1):
                if i < hops(d, h):
                    rs_step(d, h, i)
        if i == 0:
            lax.fori_loop(1, ne, gs_start, 0)
            own_gs.start()
            lax.fori_loop(0, nz, direct_build, 0)
            lax.fori_loop(1, ne, d_start, 0)
            own_d.start()
        grads(i * nz // far, (i + 1) * nz // far)
    store_in = pltpu.make_async_copy(gin, gin_hbm, st_sem.at[3])
    store_out = pltpu.make_async_copy(gout, gout_hbm, st_sem.at[4])
    store_in.start()
    store_out.start()

    def back_start(k, c):
        e = (me_e + k) % ne
        remote(back_send.at[e], back_recv.at[me_e], bk_ss.at[e], bk_rs.at[me_e], me_f, e).start()
        return c

    def back_wait(k, c):
        b = (me_e + ne - k) % ne
        remote(back_send.at[b], back_recv.at[b], bk_ss.at[b], bk_rs.at[b], me_f, b).wait_recv()
        return c

    for h in (0, 1):
        total = share(z, h)
        for d in (0, 1):
            last = hops(d, h) - 1
            rs_copy(d, h, last).wait_recv()
            total = total + rs_recv[d, h, last].astype(F32)
        back_send[h * he : (h + 1) * he] = total.astype(BF16)
    lax.fori_loop(1, ne, back_start, 0)
    own_back = pltpu.make_async_copy(back_send.at[me_e], back_recv.at[me_e], st_sem.at[5])
    own_back.start()
    direct_combine()
    gates_pass()

    def gf_wait(k, c):
        f = (me_f + nf - k) % nf
        remote(gf_all.at[f], gf_all.at[f], gf_ss.at[f], gf_rs.at[f], f, me_e).wait_recv()
        return c

    lax.fori_loop(1, nf, gf_wait, 0)
    total_gate = gf_all[0, :top, :]
    for f in range(1, nf):
        total_gate = total_gate + gf_all[f, :top, :]
    ogate_ref[...] = total_gate.astype(BF16)

    lax.fori_loop(1, nz, t_wait, 0)
    total = ts_send[z].astype(F32)
    for k in range(1, nz):
        total = total + ts_recv[(z + k) % nz].astype(F32)
    pair_send[:, :sub] = total

    lax.fori_loop(1, ne, back_wait, 0)
    own_back.wait()
    tok = tn(sel[...], flat(back_recv[...]))
    pair_send[:, sub:] = tok
    hr = rows // 2
    mine = pl.ds(pl.multiple_of(lo * hr, 16), hr)
    other = pl.ds(pl.multiple_of((1 - lo) * hr, 16), hr)
    pair = remote(pair_send.at[other], pair_recv.at[other], pr_ss, pr_rs, pair_f, me_e)
    pair.start()
    remote(pair_send.at[mine], pair_recv.at[mine], pr_ss, pr_rs, pair_f, me_e).wait_recv()
    tok_all[z, mine, :] = (pair_send[mine, :] + pair_recv[mine, :]).astype(BF16)

    def t_rows(piece, l, h):
        return tok_all.at[piece, pl.ds(pl.multiple_of(l * hr + h * (hr // 2), 16), hr // 2)]

    def t_lead(buf, piece, h):
        return t_rows(piece, lo, h)

    def swap(c, h, l):
        ref = t_rows(c, l, h)
        return remote(ref, ref, sw_ss.at[c, h], sw_rs.at[c, h], pair_f, me_e)

    def t_between(i):
        if i == 0:
            swap(z, 0, lo).start()
            swap(z, 1, lo).start()

    ring(tok_all, t_lead, tr_ss, tr_rs, t_between, lambda c, h: swap(c, h, lo).start())
    for i in range(nz):
        c = (z + (0, 1, nz - 1, 2, nz - 2, 3, nz - 3, 4)[i]) % nz if nz == 8 else i
        for h in (0, 1):
            swap(c, h, 1 - lo).wait_recv()
    for c in range(nz):
        out_ref[:, c * wz : (c + 1) * wz] = tok_all[c]

    def drain(k, c):
        e = (me_e + k) % ne
        remote(send_x.at[e], x_all.at[z, me_e], x_ss.at[e], x_rs.at[me_e], me_f, e).wait_send()
        remote(send_g.at[e], g_all.at[me_e], g_ss.at[e], g_rs.at[me_e], me_f, e).wait_send()
        remote(gs_send.at[e], gs_recv.at[me_e], gs_ss.at[e], gs_rs.at[me_e], me_f, e).wait_send()
        remote(d_send.at[e], d_recv.at[me_e], d_ss.at[e], d_rs.at[me_e], me_f, e).wait_send()
        remote(back_send.at[e], back_recv.at[me_e], bk_ss.at[e], bk_rs.at[me_e], me_f, e).wait_send()
        return c

    def drain_f(k, c):
        f = (me_f + k) % nf
        remote(gf_all.at[me_f], gf_all.at[me_f], gf_ss.at[f], gf_rs.at[me_f], f, me_e).wait_send()
        return c

    lax.fori_loop(1, ne, drain, 0)
    lax.fori_loop(1, nf, drain_f, 0)

    def drain_z(k, c):
        o = (z + k) % nz
        remote(
            ts_send.at[o], ts_recv.at[z], ts_ss.at[o], ts_rs.at[z], lo * nz + o, me_e
        ).wait_send()
        return c

    lax.fori_loop(1, nz, drain_z, 0)
    ring_drain(x_all, x_lead, xr_ss, xr_rs)
    ring_drain(tok_all, t_lead, tr_ss, tr_rs)

    def drain_swap(c, carry):
        for h in (0, 1):
            swap(c, h, lo).wait_send()
        return carry

    lax.fori_loop(0, nz, drain_swap, 0)
    for i in range(far):
        for h in (0, 1):
            for d in (0, 1):
                if i < hops(d, h):
                    rs_copy(d, h, i).wait_send()
    pair.wait_send()
    store_in.wait()
    store_out.wait()


def passing(a0, a1, a2, a3, o0, o1, o2, o3, b0, b1, b2, b3, sems):
    moves = []
    for n, (a, o, b) in enumerate(((a0, o0, b0), (a1, o1, b1), (a2, o2, b2), (a3, o3, b3))):
        pieces = PIECES if n > 1 else 1
        step = a.shape[0] // pieces
        for p in range(pieces):
            at = pl.ds(p * step, step)
            moves.append((
                pltpu.make_async_copy(a.at[at], b.at[at], sems.at[0, n, p]),
                pltpu.make_async_copy(b.at[at], o.at[at], sems.at[1, n, p]),
            ))
    for get, _ in moves:
        get.start()
    for get, put in moves:
        get.wait()
        put.start()
    for _, put in moves:
        put.wait()


def local(nf, ne, tokens, cotangent, expert_ids, gate_values, w_in, w_out):
    rows, width = tokens.shape
    top = expert_ids.shape[1]
    ff = w_in.shape[2]
    nz = nf // 2
    wz = width // nz
    far = nz // 2
    he = ne // 2
    dma = pltpu.SemaphoreType.DMA
    vmem = pl.BlockSpec(memory_space=pltpu.VMEM)
    hbm = pl.BlockSpec(memory_space=pl.ANY)
    ring_sems = dma((2, 2, far))
    out = pl.pallas_call(
        functools.partial(kernel, nf, ne),
        out_shape=(
            jax.ShapeDtypeStruct((rows, width), BF16),
            jax.ShapeDtypeStruct((top, rows), BF16),
            jax.ShapeDtypeStruct((width, ff), BF16),
            jax.ShapeDtypeStruct((ff, width), BF16),
        ),
        in_specs=[vmem, vmem, vmem, vmem, hbm, hbm],
        out_specs=(vmem, vmem, hbm, hbm),
        scratch_shapes=[
            pltpu.VMEM((width, ff), BF16),
            pltpu.VMEM((ff, width), BF16),
            pltpu.VMEM((ne, CAP, rows), F32),
            pltpu.VMEM((ne * CAP, rows), BF16),
            pltpu.VMEM((nz, ne * CAP, wz), BF16),
            pltpu.VMEM((ne * CAP, width), BF16),
            pltpu.VMEM((ne, CAP, wz), BF16),
            pltpu.VMEM((nz, ne, CAP, wz), BF16),
            pltpu.VMEM((ne, CAP, width + LANE), BF16),
            pltpu.VMEM((ne, CAP, width + LANE), BF16),
            pltpu.VMEM((ne * CAP, ff), F32),
            pltpu.VMEM((ne * CAP, ff), BF16),
            pltpu.VMEM((ne * CAP, ff), BF16),
            pltpu.VMEM((2, 2, he, CAP, wz - LANE), BF16),
            pltpu.VMEM((2, 2, far, he, CAP, wz - LANE), BF16),
            pltpu.VMEM((ne, CAP, wz - LANE), BF16),
            pltpu.VMEM((ne, CAP, wz - LANE), BF16),
            pltpu.VMEM((rows, wz), F32),
            pltpu.VMEM((rows, wz), F32),
            pltpu.VMEM((nz, rows, wz), BF16),
            pltpu.VMEM((ne, CAP, LANE), F32),
            pltpu.VMEM((ne, CAP, LANE), F32),
            pltpu.VMEM((nf, 8, rows), F32),
            pltpu.VMEM((width, ff), BF16),
            pltpu.VMEM((ff, width), BF16),
            pltpu.VMEM((ne, CAP, nz * LANE), BF16),
            pltpu.VMEM((ne, CAP, nz * LANE), BF16),
            pltpu.VMEM((nz, rows, LANE), BF16),
            pltpu.VMEM((nz, rows, LANE), BF16),
            dma((2,)),
            dma((ne,)), dma((ne,)), dma((ne,)), dma((ne,)),
            ring_sems, ring_sems, ring_sems, ring_sems,
            dma((ne,)), dma((ne,)),
            dma, dma,
            ring_sems, ring_sems,
            dma((ne,)), dma((ne,)),
            dma((nf,)), dma((nf,)),
            dma((ne,)), dma((ne,)), dma((nz,)), dma((nz,)),
            dma((nz, 2)), dma((nz, 2)),
            dma((7,)),
        ],
        compiler_params=pltpu.CompilerParams(
            collective_id=0, has_side_effects=True, vmem_limit_bytes=62 * 1024 * 1024
        ),
    )(
        tokens, cotangent, expert_ids.T, gate_values.T,
        w_in.reshape(width, ff), w_out.reshape(ff, width),
    )
    out = pl.pallas_call(
        passing,
        out_shape=tuple(jax.ShapeDtypeStruct(a.shape, a.dtype) for a in out),
        in_specs=[hbm] * 4,
        out_specs=(hbm,) * 4,
        scratch_shapes=[pltpu.VMEM(a.shape, a.dtype) for a in out] + [dma((2, 4, PIECES))],
        compiler_params=pltpu.CompilerParams(vmem_limit_bytes=62 * 1024 * 1024),
    )(*out)
    return (
        out[0],
        out[1].T,
        out[2].reshape(w_in.shape),
        out[3].reshape(w_out.shape),
    )


def solution(mesh):
    return jax.shard_map(
        functools.partial(local, mesh.shape["fsdp"], mesh.shape["expert"]),
        mesh=mesh,
        in_specs=(
            P("expert", None),
            P("expert", None),
            P("expert", None),
            P("expert", None),
            P(None, "expert", "fsdp"),
            P("fsdp", "expert", None),
        ),
        out_specs=(
            P("expert", None),
            P("expert", None),
            P(None, "expert", "fsdp"),
            P("fsdp", "expert", None),
        ),
        check_vma=False,
    )
```
